256 devices in a mesh: tok: 64 (over z_hi, x, y), head: 4 (over z_lo, core).
Axes of the slice: x: 4, y: 4, z: 8 (z_hi: 4, z_lo: 2; z = z_hi * 2 + z_lo), core: 2. Of those that a mesh axis runs over, the one named last changes fastest.
Arguments:
- queries: bfloat16 [16384, 2560], P('tok', 'head'), may hold values from -140 to 140
- keys: bfloat16 [2048, 2560], P('tok', 'head'), may hold values from -6 to 6
- values: bfloat16 [2048, 2560], P('tok', 'head'), may hold values from -6 to 6
- query_tan: bfloat16 [16384, 2560], P('tok', 'head'), may hold values from -6 to 6
- key_tan: bfloat16 [2048, 2560], P('tok', 'head'), may hold values from -6 to 6
- value_tan: bfloat16 [2048, 2560], P('tok', 'head'), may hold values from -6 to 6
- out_weight: bfloat16 [2560, 5120], P('head'), may hold values from -0.3125 to 0.3125
Outputs:
- output: bfloat16 [16384, 5120], P('tok', 'head')
- output_tan: bfloat16 [16384, 5120], P('tok', 'head')
The draws below stay inside these ranges and needn't reach their ends.
All inputs are finite; a program needn't handle non-finite values.
Results may differ from the reference program's by a relative error of at most 0.012.
Values may be sent and summed in bfloat16 or wider, within the bound.
No kernel may reach another device: no remote copies, remote signals or barrier semaphores. Data moves between devices by JAX's collectives and lax.ppermute only.
A program may use at most 128 MiB of HBM per device.

```python
import jax
import jax.numpy as jnp
from jax import lax

D = 5120
HD = 128
HEADS = 20
TOKENS = 16384
KEYS = 2048


def drawn_pair(key):
    key_draw = jnp.clip(jax.random.normal(jax.random.fold_in(key, 11), (KEYS, HEADS * HD), jnp.float32), -6.0, 6.0)
    query_draw = 2.5 * jnp.clip(jax.random.normal(jax.random.fold_in(key, 12), (TOKENS, HEADS * HD), jnp.float32), -6.0, 6.0)
    return (query_draw, key_draw)


def draw_queries(key, part):
    query_draw, key_draw = drawn_pair(key)
    return query_draw.astype(jnp.bfloat16)


def draw_keys(key, part):
    query_draw, key_draw = drawn_pair(key)
    return key_draw.astype(jnp.bfloat16)


def levels(key, shape, pieces, least, top_value):
    def one(position, blocks):
        draws = jax.random.uniform(jax.random.fold_in(jax.random.fold_in(key, 6), position), (blocks,), jnp.float32, least / len(pieces), top_value / len(pieces))
        return jnp.repeat(jnp.exp(draws), shape[position] // blocks).reshape((-1,) + (1,) * (len(shape) - position - 1))

    factor_of = one(*pieces[0])
    for cut in pieces[1:]:
        factor_of = factor_of * one(*cut)
    return factor_of


def centred(rng, extent, scale, limit, pieces=(), kind=jnp.bfloat16):
    values = scale * jax.random.normal(rng, extent, jnp.float32)
    if pieces:
        values = values * levels(rng, extent, pieces, -0.22, 0.18)
    return jnp.clip(values, -limit, limit).astype(kind)


def setup_inputs(seed: int = 0) -> dict:
    streams_of = jax.random.split(jax.random.key(seed), 8)
    queries = draw_queries(jax.random.fold_in(streams_of[7], 71), 0)
    keys = draw_keys(jax.random.fold_in(streams_of[7], 71), 0)
    values = centred(streams_of[2], (KEYS, HEADS * HD), 1.0, 6.0, ((0, 64), (1, 4)))
    query_tan = centred(streams_of[3], (TOKENS, HEADS * HD), 1.0, 6.0, ((0, 64), (1, 4)))
    key_tan = centred(streams_of[4], (KEYS, HEADS * HD), 1.0, 6.0, ((0, 64), (1, 4)))
    value_tan = centred(streams_of[5], (KEYS, HEADS * HD), 1.0, 6.0, ((0, 64), (1, 4)))
    out_weight = centred(streams_of[6], (HEADS * HD, D), (HEADS * HD // 8) ** -0.5, 0.3125, ((0, 4),))
    return dict(queries=queries, keys=keys, values=values, query_tan=query_tan, key_tan=key_tan, value_tan=value_tan, out_weight=out_weight)


def head_jvp(query_part, key_part):
    query_head, query_dir = query_part
    key_head, value_head, key_dir, value_dir = key_part
    score_scale = HD ** -0.5
    query_wide = query_head.astype(jnp.float32)
    key_wide = key_head.astype(jnp.float32)
    query_dir_wide = query_dir.astype(jnp.float32)
    key_dir_wide = key_dir.astype(jnp.float32)
    scores = jnp.dot(query_wide, key_wide.T, precision=lax.Precision.HIGHEST) * score_scale
    scores_tan = (jnp.dot(query_dir_wide, key_wide.T, precision=lax.Precision.HIGHEST)
                  + jnp.dot(query_wide, key_dir_wide.T, precision=lax.Precision.HIGHEST)) * score_scale
    row_peak = jnp.max(scores, axis=1, keepdims=True)
    exponent = jnp.exp(scores - row_peak)
    exponent_tan = exponent * scores_tan
    row_total = jnp.sum(exponent, axis=1, keepdims=True)
    row_total_tan = jnp.sum(exponent_tan, axis=1, keepdims=True)
    weights = exponent.astype(jnp.bfloat16)
    weights_tan = exponent_tan.astype(jnp.bfloat16)
    numerator = jnp.dot(weights, value_head, preferred_element_type=jnp.float32)
    numerator_tan = (jnp.dot(weights_tan, value_head, preferred_element_type=jnp.float32)
                     + jnp.dot(weights, value_dir, preferred_element_type=jnp.float32))
    attended = numerator / row_total
    attended_tan = (numerator_tan - attended * row_total_tan) / row_total
    return attended.astype(jnp.bfloat16), attended_tan.astype(jnp.bfloat16)


def split_heads(array):
    return array.reshape(array.shape[0], HEADS, HD).transpose(1, 0, 2)


def join_heads(array):
    return array.transpose(1, 0, 2).reshape(TOKENS, HEADS * HD)


def reference(queries, keys, values, query_tan, key_tan, value_tan, out_weight):
    query_parts = tuple(split_heads(array) for array in (queries, query_tan))
    key_parts = tuple(split_heads(array) for array in (keys, values, key_tan, value_tan))
    attended, attended_tan = lax.map(lambda both: head_jvp(both[0], both[1]), (query_parts, key_parts))
    output = jnp.dot(join_heads(attended), out_weight, preferred_element_type=jnp.float32)
    output_tan = jnp.dot(join_heads(attended_tan), out_weight, preferred_element_type=jnp.float32)
    return output.astype(jnp.bfloat16), output_tan.astype(jnp.bfloat16)
```

```python
import functools

import jax
import jax.numpy as jnp
from jax import lax
from jax.experimental import pallas as pl
from jax.experimental.pallas import tpu as pltpu
from jax.sharding import PartitionSpec as P

HD = 128
SCALE = HD**-0.5
EXP2_SCALE = SCALE * 1.4426950408889634
NT = (((1,), (1,)), ((), ()))
ZH, NX, NY, ZL, CORES = 4, 4, 4, 2, 2
AXES = ("tok", "head")


VMEM = pl.BlockSpec(memory_space=pltpu.VMEM)
SMEM = pl.BlockSpec(memory_space=pltpu.SMEM)
BF16 = jnp.bfloat16
F32 = jnp.float32


def shift(array, zh=0, x=0, y=0, zl=0, core=0):
    pairs = []
    for index in range(ZH * NX * NY * ZL * CORES):
        rest, c = divmod(index, CORES)
        rest, b = divmod(rest, ZL)
        rest, j = divmod(rest, NY)
        a, i = divmod(rest, NX)
        to = ((a + zh) % ZH, (i + x) % NX, (j + y) % NY, (b + zl) % ZL, (c + core) % CORES)
        target = (((to[0] * NX + to[1]) * NY + to[2]) * ZL + to[3]) * CORES + to[4]
        pairs.append((index, target))
    return lax.ppermute(array, AXES, pairs)


def across(array):
    pairs = []
    for index in range(ZH * NX * NY * ZL * CORES):
        rest, c = divmod(index, CORES)
        rest, b = divmod(rest, ZL)
        a, xy = divmod(rest, NX * NY)
        to = (a + 1) % ZH if b else (a - 1) % ZH
        pairs.append((index, ((to * NX * NY + xy) * ZL + 1 - b) * CORES + 1 - c))
    return lax.ppermute(array, AXES, pairs)


def call(kernel, outs, *operands, name, flops=0, specs=None, **kwargs):
    return pl.pallas_call(
        kernel,
        out_shape=outs,
        in_specs=specs or [VMEM] * len(operands),
        out_specs=jax.tree.map(lambda _: VMEM, outs),
        name=name,
        compiler_params=pltpu.CompilerParams(vmem_limit_bytes=48 << 20),
        cost_estimate=pl.CostEstimate(
            flops=flops,
            transcendentals=0,
            bytes_accessed=sum(o.size * o.dtype.itemsize for o in operands),
        ),
        **kwargs,
    )(*operands)


def pack_keys_kernel(k_ref, dk_ref, v_ref, dv_ref, out_ref):
    for head in range(out_ref.shape[0]):
        for slot, ref in enumerate((k_ref, dk_ref, v_ref, dv_ref)):
            out_ref[head, :, slot * HD : (slot + 1) * HD] = ref[:, head * HD : (head + 1) * HD]


def pack_queries_kernel(y_ref, q_ref, dq_ref, *out_refs):
    for k, out_ref in enumerate(out_refs):
        head = lax.rem(y_ref[0] + k, NY) if k < NY else NY
        lanes = pl.ds(pl.multiple_of(head * HD, HD), HD)
        out_ref[:, :HD] = dq_ref[:, lanes]
        out_ref[:, HD:] = q_ref[:, lanes]


def split_keys_kernel(y_ref, *refs):
    pieces, out_refs = refs[:ZH], refs[ZH:]
    for k, out_ref in enumerate(out_refs):
        head = lax.rem(y_ref[0] + k, NY) if k < NY else NY
        for z, piece in enumerate(pieces):
            rows = piece.shape[1]
            out_ref[z * rows : (z + 1) * rows, :] = piece[head]


def attend(both, key_refs, state):
    query = both[:, HD:]
    for ref in key_refs:
        keys = ref[:, : 2 * HD]
        values = ref[:, 2 * HD :]
        scores = lax.dot_general(query, keys[:, :HD], NT, preferred_element_type=F32)
        tangent = lax.dot_general(both, keys, NT, preferred_element_type=F32)
        top = jnp.max(scores, axis=1, keepdims=True)
        if state is None:
            peak = jnp.broadcast_to(top, (scores.shape[0], HD))
        else:
            peak_old, total, total_tan, numer, numer_tan = state
            peak = jnp.maximum(peak_old, top)
            fade = jnp.exp2((peak_old - peak) * EXP2_SCALE)
        expo = jnp.exp2((scores - peak[:, :1]) * EXP2_SCALE)
        expo_tan = expo * tangent
        cuts = range(0, scores.shape[1], HD)
        add = sum(expo[:, c : c + HD] for c in cuts)
        add_tan = sum(expo_tan[:, c : c + HD] for c in cuts)
        pair = jnp.dot(expo.astype(BF16), values, preferred_element_type=F32)
        single = jnp.dot(expo_tan.astype(BF16), values[:, :HD], preferred_element_type=F32)
        if state is None:
            state = (peak, add, add_tan, pair, single)
        else:
            state = (
                peak,
                total * fade + add,
                total_tan * fade + add_tan,
                numer * jnp.concatenate([fade, fade], axis=1) + pair,
                numer_tan * fade + single,
            )
    return state


def finish(state):
    _, total, total_tan, numer, numer_tan = state
    inverse = 1.0 / jnp.sum(total, axis=1, keepdims=True)
    total_tan = jnp.sum(total_tan, axis=1, keepdims=True) * SCALE
    attended = numer[:, :HD] * inverse
    attended_tan = (numer_tan * SCALE + numer[:, HD:] - attended * total_tan) * inverse
    return jnp.concatenate([attended, attended_tan], axis=1).astype(BF16)


def load_state(ref, tile):
    cut = [ref[tile, :, c * HD : (c + 1) * HD] for c in range(3)]
    return (*cut, ref[tile, :, 3 * HD : 5 * HD], ref[tile, :, 5 * HD :])


def attend_kernel(pieces, first, last, *refs):
    tiles = NY + 1
    queries, refs = refs[:tiles], refs[tiles:]
    shared, own, refs = refs[:pieces], refs[pieces : 2 * pieces], refs[2 * pieces :]
    if not first:
        state_in, refs = refs[0], refs[1:]
    for tile in range(tiles):
        state = None if first else load_state(state_in, tile)
        state = attend(queries[tile][...], shared if tile < NY else own, state)
        if last:
            refs[tile][...] = finish(state)
        else:
            refs[0][tile] = jnp.concatenate(state, axis=1)


def attend_step(queries, shared, own, state, last):
    rows = queries[0].shape[0]
    tiles = NY + 1
    keys = sum(piece.shape[0] for piece in shared)
    if last:
        outs = [jax.ShapeDtypeStruct((rows, 2 * HD), BF16)] * tiles
    else:
        outs = [jax.ShapeDtypeStruct((tiles, rows, 6 * HD), F32)]
    carried = [] if state is None else [state]
    kernel = functools.partial(attend_kernel, len(shared), state is None, last)
    found = call(
        kernel, outs, *queries, *shared, *own, *carried, name="attend", flops=tiles * rows * keys * 1792
    )
    return found if last else found[0]


def gather_heads_kernel(y_ref, *refs):
    out_ref = refs[-1]
    rows = refs[0].shape[0]
    for k, ref in enumerate(refs[:-1]):
        head = lax.rem(y_ref[0] + k, NY) if k < NY else NY
        lanes = pl.ds(pl.multiple_of(head * HD, HD), HD)
        out_ref[:rows, lanes] = ref[:, :HD]
        out_ref[rows:, lanes] = ref[:, HD:]


def project_first_kernel(c_ref, a_ref, b_ref, w_ref, u_ref, out_ref):
    del c_ref
    out_ref[...] = jnp.dot(a_ref[...], w_ref[...], preferred_element_type=F32) + jnp.dot(
        b_ref[...], u_ref[...], preferred_element_type=F32
    )


def project_last_kernel(a_ref, b_ref, w_ref, u_ref, sum_ref, out_ref, tan_ref):
    rows = out_ref.shape[0]
    total = (
        sum_ref[...]
        + jnp.dot(a_ref[...], w_ref[...], preferred_element_type=F32)
        + jnp.dot(b_ref[...], u_ref[...], preferred_element_type=F32)
    )
    out_ref[...] = total[:rows].astype(BF16)
    tan_ref[...] = total[rows:].astype(BF16)


def project(mine, sibling, weight_own, weight_core, block, columns):
    rows, depth = mine.shape
    tile = 256
    steps = columns // tile
    whole = pl.BlockSpec((rows, depth), lambda j, c: (0, 0))
    grid_spec = pltpu.PrefetchScalarGridSpec(
        num_scalar_prefetch=1,
        grid=(steps,),
        in_specs=[
            whole,
            whole,
            pl.BlockSpec((depth, tile), lambda j, c: (0, c[0] * steps + j)),
            pl.BlockSpec((depth, tile), lambda j, c: (0, j)),
        ],
        out_specs=pl.BlockSpec((rows, tile), lambda j, c: (0, j)),
    )
    return pl.pallas_call(
        project_first_kernel,
        grid_spec=grid_spec,
        out_shape=jax.ShapeDtypeStruct((rows, columns), F32),
        name="project_first",
    )(block, mine, sibling, weight_own, weight_core)


def project_rest(near, far, weight_near, weight_far, partial):
    rows, depth = near.shape
    columns = partial.shape[1]
    tile = 256
    whole = pl.BlockSpec((rows, depth), lambda j: (0, 0))
    cut = pl.BlockSpec((depth, tile), lambda j: (0, j))
    half = pl.BlockSpec((rows // 2, tile), lambda j: (0, j))
    return pl.pallas_call(
        project_last_kernel,
        grid=(columns // tile,),
        in_specs=[whole, whole, cut, cut, pl.BlockSpec((rows, tile), lambda j: (0, j))],
        out_specs=[half, half],
        out_shape=[jax.ShapeDtypeStruct((rows // 2, columns), BF16)] * 2,
        name="project_last",
    )(near, far, weight_near, weight_far, partial)


def shards(queries, keys, values, query_tan, key_tan, value_tan, out_weight):
    rows, width = queries.shape
    heads = width // HD
    slab = keys.shape[0]
    columns = out_weight.shape[1] // (ZL * CORES)
    y = (lax.axis_index("tok") % NY).astype(jnp.int32).reshape(1)
    place = lax.axis_index("head").astype(jnp.int32)
    with_index = [SMEM] + [VMEM] * 8

    packed = call(
        pack_keys_kernel,
        jax.ShapeDtypeStruct((heads, slab, 4 * HD), BF16),
        keys,
        key_tan,
        values,
        value_tan,
        name="pack_keys",
    )
    pieces = [packed] + [shift(packed, zh=k) for k in (1, 3, 2)]

    sends = call(
        pack_queries_kernel,
        [jax.ShapeDtypeStruct((rows, 2 * HD), BF16)] * (NY + 1),
        y,
        queries,
        query_tan,
        name="pack_queries",
        specs=with_index[:3],
    )
    blocks = [sends[0]] + [shift(sends[k], y=k) for k in (1, 2, 3)] + [sends[NY]]

    split = call(
        split_keys_kernel,
        [jax.ShapeDtypeStruct((ZH * slab, 4 * HD), BF16)] * (NY + 1),
        y,
        *pieces,
        name="split_keys",
        specs=with_index[: ZH + 1],
    )
    shared = jnp.concatenate([split[0]] + [shift(split[k], y=k) for k in (1, 3, 2)])
    own = jnp.concatenate([split[NY]] + [shift(split[NY], x=k) for k in (1, 3, 2)])
    shared_far = [shift(shared, x=k) for k in (1, 3, 2)]
    own_far = [shift(own, y=k) for k in (1, 3, 2)]

    weight, _ = lax.optimization_barrier((out_weight, split[0]))

    def cut(block):
        return lax.dynamic_slice(weight, (0, block * columns), (weight.shape[0], columns))

    weight_core = shift(cut(place ^ 1), core=1)
    weight_near = shift(cut(place ^ 2), zl=1)
    weight_far = across(cut(place ^ 3))

    state = attend_step(blocks, [shared], [own], None, False)
    state = attend_step(blocks, shared_far[:2], own_far[:2], state, False)
    done = attend_step(blocks, shared_far[2:], own_far[2:], state, True)

    back = [done[0]] + [shift(done[k], y=-k) for k in (1, 2, 3)] + [done[NY]]
    mine = call(
        gather_heads_kernel,
        jax.ShapeDtypeStruct((2 * rows, width), BF16),
        y,
        *back,
        name="gather_heads",
        specs=with_index[: NY + 2],
    )
    near = shift(mine, zl=1)
    sibling = shift(mine, core=1)
    far = shift(near, core=1)
    partial = project(mine, sibling, out_weight, weight_core, place.reshape(1), columns)
    return tuple(project_rest(near, far, weight_near, weight_far, partial))


def solution(mesh):
    spec = P("tok", "head")
    return jax.shard_map(
        shards,
        mesh=mesh,
        in_specs=(spec,) * 6 + (P("head", None),),
        out_specs=(spec, spec),
        check_vma=False,
    )
```

```python
import functools

import jax
import jax.numpy as jnp
from jax import lax
from jax.experimental import pallas as pl
from jax.experimental.pallas import tpu as pltpu
from jax.sharding import PartitionSpec as P


HD = 128
SCALE = HD**-0.5
EXP2_SCALE = SCALE * 1.4426950408889634
NT = (((1,), (1,)), ((), ()))
ZH, NX, NY, ZL, CORES = 4, 4, 4, 2, 2
AXES = ("tok", "head")


VMEM = pl.BlockSpec(memory_space=pltpu.VMEM)
SMEM = pl.BlockSpec(memory_space=pltpu.SMEM)
HBM = pl.BlockSpec(memory_space=pltpu.HBM)
BF16 = jnp.bfloat16
F32 = jnp.float32


def shift(array, zh=0, x=0, y=0, zl=0, core=0):
    pairs = []
    for index in range(ZH * NX * NY * ZL * CORES):
        rest, c = divmod(index, CORES)
        rest, b = divmod(rest, ZL)
        rest, j = divmod(rest, NY)
        a, i = divmod(rest, NX)
        to = ((a + zh) % ZH, (i + x) % NX, (j + y) % NY, (b + zl) % ZL, (c + core) % CORES)
        target = (((to[0] * NX + to[1]) * NY + to[2]) * ZL + to[3]) * CORES + to[4]
        pairs.append((index, target))
    return lax.ppermute(array, AXES, pairs)


def across(array):
    pairs = []
    for index in range(ZH * NX * NY * ZL * CORES):
        rest, c = divmod(index, CORES)
        rest, b = divmod(rest, ZL)
        a, xy = divmod(rest, NX * NY)
        to = (a + 1) % ZH if b else (a - 1) % ZH
        pairs.append((index, ((to * NX * NY + xy) * ZL + 1 - b) * CORES + 1 - c))
    return lax.ppermute(array, AXES, pairs)


def call(kernel, outs, *operands, flops=0, specs=None, limit=16, **kwargs):
    return called(kernel, outs, operands, flops, specs, limit, kwargs)


def called(kernel, outs, operands, flops, specs, limit, kwargs):
    return pl.pallas_call(
        kernel,
        out_shape=outs,
        in_specs=specs or [VMEM] * len(operands),
        out_specs=jax.tree.map(lambda _: VMEM, outs),
        compiler_params=pltpu.CompilerParams(vmem_limit_bytes=limit << 20),
        cost_estimate=pl.CostEstimate(
            flops=flops,
            transcendentals=0,
            bytes_accessed=sum(o.size * o.dtype.itemsize for o in operands),
        ),
        **kwargs,
    )(*operands)


def fetch(source_refs, held_ref, sems):
    copies = [
        pltpu.make_async_copy(ref, held_ref.at[slot], sems.at[slot]) for slot, ref in enumerate(source_refs)
    ]
    for copy in copies:
        copy.start()
    for copy in copies:
        copy.wait()


def pack_keys_kernel(k_ref, dk_ref, v_ref, dv_ref, out_ref, held_ref, sems):
    fetch((k_ref, dk_ref, v_ref, dv_ref), held_ref, sems)
    for head in range(out_ref.shape[0]):
        for slot in range(4):
            out_ref[head, :, slot * HD : (slot + 1) * HD] = held_ref[slot, :, head * HD : (head + 1) * HD]


def pack_queries_kernel(y_ref, q_ref, dq_ref, *refs):
    out_refs, (held_ref, sems) = refs[:-2], refs[-2:]
    fetch((dq_ref, q_ref), held_ref, sems)
    for k, out_ref in enumerate(out_refs):
        head = lax.rem(y_ref[0] + k, NY) if k < NY else NY
        lanes = pl.ds(pl.multiple_of(head * HD, HD), HD)
        out_ref[:, :HD] = held_ref[0, :, lanes]
        out_ref[:, HD:] = held_ref[1, :, lanes]


def split_keys_kernel(y_ref, *refs):
    pieces, out_refs = refs[:ZH], refs[ZH:]
    for k, out_ref in enumerate(out_refs):
        head = lax.rem(y_ref[0] + k, NY) if k < NY else NY
        for z, piece in enumerate(pieces):
            rows = piece.shape[1]
            out_ref[z * rows : (z + 1) * rows, :] = piece[head]


def attend(both, key_refs, state):
    query = both[:, HD:]
    for ref in key_refs:
        keys = ref[:, : 2 * HD]
        values = ref[:, 2 * HD :]
        scores = lax.dot_general(query, keys[:, :HD], NT, preferred_element_type=F32)
        tangent = lax.dot_general(both, keys, NT, preferred_element_type=F32)
        top = jnp.max(scores, axis=1, keepdims=True)
        if state is None:
            peak = jnp.broadcast_to(top, (scores.shape[0], HD))
        else:
            peak_old, total, total_tan, numer, numer_tan = state
            peak = jnp.maximum(peak_old, top)
            fade = jnp.exp2((peak_old - peak) * EXP2_SCALE)
        expo = jnp.exp2((scores - peak[:, :1]) * EXP2_SCALE)
        expo_tan = expo * tangent
        cuts = range(0, scores.shape[1], HD)
        add = sum(expo[:, c : c + HD] for c in cuts)
        add_tan = sum(expo_tan[:, c : c + HD] for c in cuts)
        pair = jnp.dot(expo.astype(BF16), values, preferred_element_type=F32)
        single = jnp.dot(expo_tan.astype(BF16), values[:, :HD], preferred_element_type=F32)
        if state is None:
            state = (peak, add, add_tan, pair, single)
        else:
            state = (
                peak,
                total * fade + add,
                total_tan * fade + add_tan,
                numer * jnp.concatenate([fade, fade], axis=1) + pair,
                numer_tan * fade + single,
            )
    return state


def finish(state):
    _, total, total_tan, numer, numer_tan = state
    inverse = 1.0 / jnp.sum(total, axis=1, keepdims=True)
    total_tan = jnp.sum(total_tan, axis=1, keepdims=True) * SCALE
    attended = numer[:, :HD] * inverse
    attended_tan = (numer_tan * SCALE + numer[:, HD:] - attended * total_tan) * inverse
    return jnp.concatenate([attended, attended_tan], axis=1).astype(BF16)


def load_state(ref, tile):
    cut = [ref[tile, :, c * HD : (c + 1) * HD] for c in range(3)]
    return (*cut, ref[tile, :, 3 * HD : 5 * HD], ref[tile, :, 5 * HD :])


def attend_kernel(pieces, first, last, *refs):
    tiles = NY + 1
    queries, refs = refs[:tiles], refs[tiles:]
    shared, own, refs = refs[:pieces], refs[pieces : 2 * pieces], refs[2 * pieces :]
    if not first:
        state_in, refs = refs[0], refs[1:]
    for tile in range(tiles):
        state = None if first else load_state(state_in, tile)
        state = attend(queries[tile][...], shared if tile < NY else own, state)
        if last:
            refs[tile][...] = finish(state)
        else:
            refs[0][tile] = jnp.concatenate(state, axis=1)


def attend_step(queries, shared, own, state, last):
    rows = queries[0].shape[0]
    tiles = NY + 1
    keys = sum(piece.shape[0] for piece in shared)
    if last:
        outs = [jax.ShapeDtypeStruct((rows, 2 * HD), BF16)] * tiles
    else:
        outs = [jax.ShapeDtypeStruct((tiles, rows, 6 * HD), F32)]
    carried = [] if state is None else [state]
    kernel = functools.partial(attend_kernel, len(shared), state is None, last)
    found = call(kernel, outs, *queries, *shared, *own, *carried, flops=tiles * rows * keys * 1792)
    return found if last else found[0]


def gather_heads_kernel(y_ref, *refs):
    out_ref = refs[-1]
    rows = refs[0].shape[0]
    for k, ref in enumerate(refs[:-1]):
        head = lax.rem(y_ref[0] + k, NY) if k < NY else NY
        lanes = pl.ds(pl.multiple_of(head * HD, HD), HD)
        out_ref[:rows, lanes] = ref[:, :HD]
        out_ref[rows:, lanes] = ref[:, HD:]


def project_first_kernel(a_ref, b_ref, w_ref, u_ref, out_ref):
    out_ref[...] = jnp.dot(a_ref[...], w_ref[...], preferred_element_type=F32) + jnp.dot(
        b_ref[...], u_ref[...], preferred_element_type=F32
    )


def project_last_kernel(a_ref, b_ref, w_ref, u_ref, sum_ref, out_ref, tan_ref):
    rows, tile = out_ref.shape
    lanes = pl.ds(pl.multiple_of(pl.program_id(0) * tile, tile), tile)
    for ref, half in ((out_ref, pl.ds(0, rows)), (tan_ref, pl.ds(rows, rows))):
        total = (
            sum_ref[half, lanes]
            + jnp.dot(a_ref[half, :], w_ref[:, lanes], preferred_element_type=F32)
            + jnp.dot(b_ref[half, :], u_ref[:, lanes], preferred_element_type=F32)
        )
        ref[...] = total.astype(BF16)


def project_last(near, far, weight_near, weight_far, partial):
    rows, columns = partial.shape
    tile = 256
    half = pl.BlockSpec((rows // 2, tile), lambda j: (0, j))
    return pl.pallas_call(
        project_last_kernel,
        grid=(columns // tile,),
        in_specs=[VMEM] * 5,
        out_specs=[half, half],
        out_shape=[jax.ShapeDtypeStruct((rows // 2, columns), BF16)] * 2,
        name="project_last",
        compiler_params=pltpu.CompilerParams(vmem_limit_bytes=16 << 20),
    )(near, far, weight_near, weight_far, partial)


def shard_step(queries, keys, values, query_tan, key_tan, value_tan, out_weight):
    rows, width = queries.shape
    heads = width // HD
    slab = keys.shape[0]
    columns = out_weight.shape[1] // (ZL * CORES)
    y = (lax.axis_index("tok") % NY).astype(jnp.int32).reshape(1)
    place = lax.axis_index("head").astype(jnp.int32)
    with_index = [SMEM] + [VMEM] * 8

    keys, values, query_tan, key_tan, value_tan, queries = (
        pltpu.with_memory_space_constraint(array, pltpu.HBM)
        for array in (keys, values, query_tan, key_tan, value_tan, queries)
    )

    packed = call(
        pack_keys_kernel,
        jax.ShapeDtypeStruct((heads, slab, 4 * HD), BF16),
        keys,
        key_tan,
        values,
        value_tan,
        specs=[HBM] * 4,
        scratch_shapes=[pltpu.VMEM((4, slab, width), BF16), pltpu.SemaphoreType.DMA((4,))],
    )
    pieces = [packed] + [shift(packed, zh=k) for k in (1, 3, 2)]

    sends = call(
        pack_queries_kernel,
        [jax.ShapeDtypeStruct((rows, 2 * HD), BF16)] * (NY + 1),
        y,
        queries,
        query_tan,
        specs=[SMEM, HBM, HBM],
        scratch_shapes=[pltpu.VMEM((2, rows, width), BF16), pltpu.SemaphoreType.DMA((2,))],
    )
    blocks = [sends[0]] + [shift(sends[k], y=k) for k in (1, 2, 3)] + [sends[NY]]

    weight, _ = lax.optimization_barrier((out_weight, sends[1]))
    cuts = [
        lax.dynamic_slice(weight, (0, (place ^ k) * columns), (weight.shape[0], columns))
        for k in range(ZL * CORES)
    ]
    pieces, cuts = lax.optimization_barrier((pieces, cuts))

    split = call(
        split_keys_kernel,
        [jax.ShapeDtypeStruct((ZH * slab, 4 * HD), BF16)] * (NY + 1),
        y,
        *pieces,
        specs=with_index[: ZH + 1],
    )
    shared = jnp.concatenate([split[0]] + [shift(split[k], y=k) for k in (1, 3, 2)])
    own = jnp.concatenate([split[NY]] + [shift(split[NY], x=k) for k in (1, 3, 2)])
    shared_far = [shift(shared, x=k) for k in (1, 3, 2)]
    own_far = [shift(own, y=k) for k in (1, 3, 2)]

    cuts, _ = lax.optimization_barrier((cuts, split[0]))
    weight_core = shift(cuts[1], core=1)
    weight_near = shift(cuts[2], zl=1)
    weight_far = across(cuts[3])

    state = attend_step(blocks, [shared], [own], None, False)
    state = attend_step(blocks, shared_far[:1], own_far[:1], state, False)
    state = attend_step(blocks, shared_far[1:2], own_far[1:2], state, False)
    done = attend_step(blocks, shared_far[2:], own_far[2:], state, True)

    back = [done[0]] + [shift(done[k], y=-k) for k in (1, 2, 3)] + [done[NY]]
    mine = call(
        gather_heads_kernel,
        jax.ShapeDtypeStruct((2 * rows, width), BF16),
        y,
        *back,
        specs=with_index[: NY + 2],
    )
    near = shift(mine, zl=1)
    sibling = shift(mine, core=1)
    partial = call(
        project_first_kernel,
        jax.ShapeDtypeStruct((2 * rows, columns), F32),
        mine,
        sibling,
        cuts[0],
        weight_core,
        flops=8 * rows * width * columns,
    )
    near, partial = lax.optimization_barrier((near, partial))
    far = shift(near, core=1)
    return tuple(project_last(near, far, weight_near, weight_far, partial))


def solution(mesh):
    spec = P("tok", "head")
    return jax.shard_map(
        shard_step,
        mesh=mesh,
        in_specs=(spec,) * 6 + (P("head", None),),
        out_specs=(spec, spec),
        check_vma=False,
    )
```

```python
import functools

import jax
import jax.numpy as jnp
from jax import lax
from jax.experimental import pallas as pl
from jax.experimental.pallas import tpu as pltpu
from jax.sharding import PartitionSpec as P


HD = 128
SCALE = HD**-0.5
EXP2_SCALE = SCALE * 1.4426950408889634
NT = (((1,), (1,)), ((), ()))
ZH, NX, NY, ZL, CORES = 4, 4, 4, 2, 2
SLOTS = (0, NY, 1, 2, 3)
AXES = ("tok", "head")


VMEM = pl.BlockSpec(memory_space=pltpu.VMEM)
SMEM = pl.BlockSpec(memory_space=pltpu.SMEM)
HBM = pl.BlockSpec(memory_space=pltpu.HBM)
BF16 = jnp.bfloat16
F32 = jnp.float32


def shift(array, zh=0, x=0, y=0, zl=0, core=0):
    pairs = []
    for index in range(ZH * NX * NY * ZL * CORES):
        rest, c = divmod(index, CORES)
        rest, b = divmod(rest, ZL)
        rest, j = divmod(rest, NY)
        a, i = divmod(rest, NX)
        to = ((a + zh) % ZH, (i + x) % NX, (j + y) % NY, (b + zl) % ZL, (c + core) % CORES)
        target = (((to[0] * NX + to[1]) * NY + to[2]) * ZL + to[3]) * CORES + to[4]
        pairs.append((index, target))
    return lax.ppermute(array, AXES, pairs)


def across(array):
    pairs = []
    for index in range(ZH * NX * NY * ZL * CORES):
        rest, c = divmod(index, CORES)
        rest, b = divmod(rest, ZL)
        a, xy = divmod(rest, NX * NY)
        to = (a + 1) % ZH if b else (a - 1) % ZH
        pairs.append((index, ((to * NX * NY + xy) * ZL + 1 - b) * CORES + 1 - c))
    return lax.ppermute(array, AXES, pairs)


def call(kernel, outs, *operands, flops=0, specs=None, limit=16, **kwargs):
    return called(kernel, outs, operands, flops, specs, limit, kwargs)


def called(kernel, outs, operands, flops, specs, limit, kwargs):
    return pl.pallas_call(
        kernel,
        out_shape=outs,
        in_specs=specs or [VMEM] * len(operands),
        out_specs=jax.tree.map(lambda _: VMEM, outs),
        compiler_params=pltpu.CompilerParams(vmem_limit_bytes=limit << 20),
        cost_estimate=pl.CostEstimate(
            flops=flops,
            transcendentals=0,
            bytes_accessed=sum(o.size * o.dtype.itemsize for o in operands),
        ),
        **kwargs,
    )(*operands)


def fetch(source_refs, held_ref, sems):
    copies = [
        pltpu.make_async_copy(ref, held_ref.at[slot], sems.at[slot]) for slot, ref in enumerate(source_refs)
    ]
    for copy in copies:
        copy.start()
    for copy in copies:
        copy.wait()


def pack_keys_kernel(k_ref, dk_ref, v_ref, dv_ref, out_ref, held_ref, sems):
    fetch((k_ref, dk_ref, v_ref, dv_ref), held_ref, sems)
    for head in range(out_ref.shape[0]):
        for slot in range(4):
            out_ref[head, :, slot * HD : (slot + 1) * HD] = held_ref[slot, :, head * HD : (head + 1) * HD]


def pack_queries_kernel(y_ref, q_ref, dq_ref, *refs):
    out_refs, (held_ref, sems) = refs[:-2], refs[-2:]
    fetch((dq_ref, q_ref), held_ref, sems)
    for k, out_ref in enumerate(out_refs):
        head = lax.rem(y_ref[0] + k, NY) if k < NY else NY
        lanes = pl.ds(pl.multiple_of(head * HD, HD), HD)
        out_ref[:, :HD] = held_ref[0, :, lanes]
        out_ref[:, HD:] = held_ref[1, :, lanes]


def split_keys_kernel(y_ref, *refs):
    pieces, out_refs = refs[:ZH], refs[ZH:]
    for k, out_ref in enumerate(out_refs):
        head = lax.rem(y_ref[0] + k, NY) if k < NY else NY
        for z, piece in enumerate(pieces):
            rows = piece.shape[1]
            out_ref[z * rows : (z + 1) * rows, :] = piece[head]


def attend(both, key_refs, state):
    query = both[:, HD:]
    for ref in key_refs:
        keys = ref[:, : 2 * HD]
        values = ref[:, 2 * HD :]
        scores = lax.dot_general(query, keys[:, :HD], NT, preferred_element_type=F32)
        tangent = lax.dot_general(both, keys, NT, preferred_element_type=F32)
        top = jnp.max(scores, axis=1, keepdims=True)
        if state is None:
            peak = jnp.broadcast_to(top, (scores.shape[0], HD))
        else:
            peak_old, total, total_tan, numer, numer_tan = state
            peak = jnp.maximum(peak_old, top)
            fade = jnp.exp2((peak_old - peak) * EXP2_SCALE)
        expo = jnp.exp2((scores - peak[:, :1]) * EXP2_SCALE)
        expo_tan = expo * tangent
        cuts = range(0, scores.shape[1], HD)
        add = sum(expo[:, c : c + HD] for c in cuts)
        add_tan = sum(expo_tan[:, c : c + HD] for c in cuts)
        pair = jnp.dot(expo.astype(BF16), values, preferred_element_type=F32)
        single = jnp.dot(expo_tan.astype(BF16), values[:, :HD], preferred_element_type=F32)
        if state is None:
            state = (peak, add, add_tan, pair, single)
        else:
            state = (
                peak,
                total * fade + add,
                total_tan * fade + add_tan,
                numer * jnp.concatenate([fade, fade], axis=1) + pair,
                numer_tan * fade + single,
            )
    return state


def finish(state):
    _, total, total_tan, numer, numer_tan = state
    inverse = 1.0 / jnp.sum(total, axis=1, keepdims=True)
    total_tan = jnp.sum(total_tan, axis=1, keepdims=True) * SCALE
    attended = numer[:, :HD] * inverse
    attended_tan = (numer_tan * SCALE + numer[:, HD:] - attended * total_tan) * inverse
    return jnp.concatenate([attended, attended_tan], axis=0).astype(BF16)


def load_state(ref, tile):
    cut = [ref[tile, :, c * HD : (c + 1) * HD] for c in range(3)]
    return (*cut, ref[tile, :, 3 * HD : 5 * HD], ref[tile, :, 5 * HD :])


def attend_kernel(tiles, first, joined, *refs):
    queries, refs = refs[: len(tiles)], refs[len(tiles) :]
    (shared, own), refs = refs[:2], refs[2:]
    if not first:
        state_in, refs = refs[0], refs[1:]
    for place, tile in enumerate(tiles):
        state = None if first else load_state(state_in, tile)
        state = attend(queries[place][...], [shared if tile < NY else own], state)
        if joined is None:
            refs[0][tile] = jnp.concatenate(state, axis=1)
        elif joined:
            refs[0][:, place * HD : (place + 1) * HD] = finish(state)
        else:
            refs[place][...] = finish(state)


def attend_step(blocks, shared, own, state, tiles=tuple(range(NY + 1)), joined=None):
    rows = blocks[0].shape[0]
    if joined is None:
        outs = [jax.ShapeDtypeStruct((NY + 1, rows, 6 * HD), F32)]
    elif joined:
        outs = [jax.ShapeDtypeStruct((2 * rows, len(tiles) * HD), BF16)]
    else:
        outs = [jax.ShapeDtypeStruct((2 * rows, HD), BF16)] * len(tiles)
    carried = [] if state is None else [state]
    found = call(
        functools.partial(attend_kernel, tiles, state is None, joined),
        outs,
        *[blocks[tile] for tile in tiles],
        shared,
        own,
        *carried,
        flops=len(tiles) * rows * shared.shape[0] * 1792,
    )
    return found if joined is False else found[0]


def cut_weight_kernel(y_ref, place_ref, w_ref, *refs):
    out_refs, sems = refs[:-1], refs[-1]
    columns = out_refs[0].shape[1]
    copies = []
    for flip, out_ref in enumerate(out_refs):
        block = lax.bitwise_xor(place_ref[0], flip)
        lanes = pl.ds(pl.multiple_of(block * columns, HD), columns)
        for slot, k in enumerate(SLOTS):
            head = lax.rem(y_ref[0] + k, NY) if k < NY else NY
            source = w_ref.at[pl.ds(pl.multiple_of(head * HD, HD), HD), lanes]
            target = out_ref.at[slot * HD : (slot + 1) * HD]
            copies.append(pltpu.make_async_copy(source, target, sems.at[flip, slot]))
    for copy in copies:
        copy.start()
    for copy in copies:
        copy.wait()


def project_first_kernel(*refs):
    weights, out_ref = refs[6:10], refs[10]
    own, far_rows = 2 * HD, 5 * HD
    total = None
    for ref, weight, low, high in (
        (refs[0], weights[0], 0, own),
        (refs[1], weights[0], own, far_rows),
        (refs[2], weights[1], 0, own),
        (refs[3], weights[1], own, far_rows),
        (refs[4], weights[2], 0, own),
        (refs[5], weights[3], 0, own),
    ):
        part = jnp.dot(ref[...], weight[low:high, :], preferred_element_type=F32)
        total = part if total is None else total + part
    out_ref[...] = total


def project_last_kernel(a_ref, b_ref, w_ref, u_ref, sum_ref, out_ref, tan_ref):
    rows, tile = out_ref.shape
    depth = a_ref.shape[1]
    lanes = pl.ds(pl.multiple_of(pl.program_id(0) * tile, tile), tile)
    weights = pl.ds(w_ref.shape[0] - depth, depth)
    for ref, half in ((out_ref, pl.ds(0, rows)), (tan_ref, pl.ds(rows, rows))):
        total = (
            sum_ref[half, lanes]
            + jnp.dot(a_ref[half, :], w_ref[weights, lanes], preferred_element_type=F32)
            + jnp.dot(b_ref[half, :], u_ref[weights, lanes], preferred_element_type=F32)
        )
        ref[...] = total.astype(BF16)


def project_last(near, far, weight_near, weight_far, partial):
    rows, columns = partial.shape
    tile = 256
    half = pl.BlockSpec((rows // 2, tile), lambda j: (0, j))
    return pl.pallas_call(
        project_last_kernel,
        grid=(columns // tile,),
        in_specs=[VMEM] * 5,
        out_specs=[half, half],
        out_shape=[jax.ShapeDtypeStruct((rows // 2, columns), BF16)] * 2,
        name="project_last",
        compiler_params=pltpu.CompilerParams(vmem_limit_bytes=16 << 20),
    )(near, far, weight_near, weight_far, partial)


def shard_step(queries, keys, values, query_tan, key_tan, value_tan, out_weight):
    rows, width = queries.shape
    heads = width // HD
    slab = keys.shape[0]
    columns = out_weight.shape[1] // (ZL * CORES)
    y = (lax.axis_index("tok") % NY).astype(jnp.int32).reshape(1)
    place = lax.axis_index("head").astype(jnp.int32).reshape(1)
    with_index = [SMEM] + [VMEM] * 8
    out_weight = pltpu.with_memory_space_constraint(out_weight, pltpu.HBM)
    keys, values, query_tan, key_tan, value_tan, queries = (
        pltpu.with_memory_space_constraint(array, pltpu.HBM)
        for array in (keys, values, query_tan, key_tan, value_tan, queries)
    )

    packed = call(
        pack_keys_kernel,
        jax.ShapeDtypeStruct((heads, slab, 4 * HD), BF16),
        keys,
        key_tan,
        values,
        value_tan,
        specs=[HBM] * 4,
        scratch_shapes=[pltpu.VMEM((4, slab, width), BF16), pltpu.SemaphoreType.DMA((4,))],
    )
    pieces = [packed] + [shift(packed, zh=k) for k in (1, 3, 2)]

    sends = call(
        pack_queries_kernel,
        [jax.ShapeDtypeStruct((rows, 2 * HD), BF16)] * (NY + 1),
        y,
        queries,
        query_tan,
        specs=[SMEM, HBM, HBM],
        scratch_shapes=[pltpu.VMEM((2, rows, width), BF16), pltpu.SemaphoreType.DMA((2,))],
    )
    blocks = [sends[0]] + [shift(sends[k], y=k) for k in (1, 2, 3)] + [sends[NY]]

    place, _ = lax.optimization_barrier((place, sends[1]))
    cuts = call(
        cut_weight_kernel,
        [jax.ShapeDtypeStruct((width, columns), BF16)] * (ZL * CORES),
        y,
        place,
        out_weight,
        specs=[SMEM, SMEM, HBM],
        scratch_shapes=[pltpu.SemaphoreType.DMA((ZL * CORES, NY + 1))],
    )
    pieces, cuts = lax.optimization_barrier((pieces, cuts))

    split = call(
        split_keys_kernel,
        [jax.ShapeDtypeStruct((ZH * slab, 4 * HD), BF16)] * (NY + 1),
        y,
        *pieces,
        specs=with_index[: ZH + 1],
    )
    shared = jnp.concatenate([split[0]] + [shift(split[k], y=k) for k in (1, 3, 2)])
    own = jnp.concatenate([split[NY]] + [shift(split[NY], x=k) for k in (1, 3, 2)])
    shared_far = [shift(shared, x=k) for k in (1, 3, 2)]
    own_far = [shift(own, y=k) for k in (1, 3, 2)]

    cuts, _ = lax.optimization_barrier((cuts, split[0]))
    weight_core = shift(cuts[1], core=1)
    weight_near = shift(cuts[2], zl=1)
    weight_far = across(cuts[3])

    state = attend_step(blocks, shared, own, None)
    for k in range(2):
        state = attend_step(blocks, shared_far[k], own_far[k], state)
    others = attend_step(blocks, shared_far[2], own_far[2], state, (1, 2, 3), False)
    own_far[2], _ = lax.optimization_barrier((own_far[2], others[0]))
    mine = [attend_step(blocks, shared_far[2], own_far[2], state, (0, NY), True)]
    back = [shift(others[k - 1], y=-k) for k in (1, 2, 3)]
    mine.append(jnp.concatenate(back, axis=1))

    near = [shift(mine[n], zl=1) for n in range(2)]
    sibling = [shift(mine[n], core=1) for n in range(2)]
    far = shift(near[0], core=1)
    partial = call(
        project_first_kernel,
        jax.ShapeDtypeStruct((2 * rows, columns), F32),
        *mine,
        *sibling,
        near[0],
        far,
        cuts[0],
        weight_core,
        weight_near,
        weight_far,
        flops=10 * rows * width * columns,
    )
    last, partial = lax.optimization_barrier((near[1], partial))
    far = shift(last, core=1)
    return tuple(project_last(last, far, weight_near, weight_far, partial))


def solution(mesh):
    spec = P("tok", "head")
    return jax.shard_map(
        shard_step,
        mesh=mesh,
        in_specs=(spec,) * 6 + (P("head", None),),
        out_specs=(spec, spec),
        check_vma=False,
    )
```

```python
import functools

import jax
import jax.numpy as jnp
from jax import lax
from jax.experimental import pallas as pl
from jax.experimental.pallas import tpu as pltpu
from jax.sharding import PartitionSpec as P


HD = 128
SCALE = HD**-0.5
EXP2_SCALE = SCALE * 1.4426950408889634
NT = (((1,), (1,)), ((), ()))
ZH, NX, NY, ZL, CORES = 4, 4, 4, 2, 2
SLOTS = (0, NY, 1, 2, 3)
AXES = ("tok", "head")


VMEM = pl.BlockSpec(memory_space=pltpu.VMEM)
SMEM = pl.BlockSpec(memory_space=pltpu.SMEM)
HBM = pl.BlockSpec(memory_space=pltpu.HBM)
BF16 = jnp.bfloat16
F32 = jnp.float32


def shift(array, zh=0, swap=0, ring=0, zl=0, core=0):
    pairs = []
    for index in range(ZH * NX * NY * ZL * CORES):
        rest, c = divmod(index, CORES)
        rest, b = divmod(rest, ZL)
        rest, j = divmod(rest, NY)
        a, i = divmod(rest, NX)
        x, y = (swap, ring) if c else (ring, swap)
        to = ((a + zh) % ZH, (i + x) % NX, (j + y) % NY, (b + zl) % ZL, (c + core) % CORES)
        target = (((to[0] * NX + to[1]) * NY + to[2]) * ZL + to[3]) * CORES + to[4]
        pairs.append((index, target))
    return lax.ppermute(array, AXES, pairs)


def across(array):
    pairs = []
    for index in range(ZH * NX * NY * ZL * CORES):
        rest, c = divmod(index, CORES)
        rest, b = divmod(rest, ZL)
        a, xy = divmod(rest, NX * NY)
        to = (a + 1) % ZH if b else (a - 1) % ZH
        pairs.append((index, ((to * NX * NY + xy) * ZL + 1 - b) * CORES + 1 - c))
    return lax.ppermute(array, AXES, pairs)


def call(kernel, outs, *operands, flops=0, specs=None, limit=16, **kwargs):
    return called(kernel, outs, operands, flops, specs, limit, kwargs)


def called(kernel, outs, operands, flops, specs, limit, kwargs):
    return pl.pallas_call(
        kernel,
        out_shape=outs,
        in_specs=specs or [VMEM] * len(operands),
        out_specs=jax.tree.map(lambda _: VMEM, outs),
        compiler_params=pltpu.CompilerParams(vmem_limit_bytes=limit << 20),
        cost_estimate=pl.CostEstimate(
            flops=flops,
            transcendentals=0,
            bytes_accessed=sum(o.size * o.dtype.itemsize for o in operands),
        ),
        **kwargs,
    )(*operands)


def fetch(source_refs, held_ref, sems):
    copies = [
        pltpu.make_async_copy(ref, held_ref.at[slot], sems.at[slot]) for slot, ref in enumerate(source_refs)
    ]
    for copy in copies:
        copy.start()
    for copy in copies:
        copy.wait()


def pack_keys_kernel(k_ref, dk_ref, v_ref, dv_ref, out_ref, held_ref, sems):
    fetch((k_ref, dk_ref, v_ref, dv_ref), held_ref, sems)
    for head in range(out_ref.shape[0]):
        for slot in range(4):
            out_ref[head, :, slot * HD : (slot + 1) * HD] = held_ref[slot, :, head * HD : (head + 1) * HD]


def pack_queries_kernel(y_ref, q_ref, dq_ref, *refs):
    out_refs, (held_ref, sems) = refs[:-2], refs[-2:]
    fetch((dq_ref, q_ref), held_ref, sems)
    for k, out_ref in enumerate(out_refs):
        head = lax.rem(y_ref[0] + k, NY) if k < NY else NY
        lanes = pl.ds(pl.multiple_of(head * HD, HD), HD)
        out_ref[:, :HD] = held_ref[0, :, lanes]
        out_ref[:, HD:] = held_ref[1, :, lanes]


def split_keys_kernel(y_ref, *refs):
    pieces, out_refs = refs[:ZH], refs[ZH:]
    for k, out_ref in enumerate(out_refs):
        for half, head in enumerate((lax.rem(y_ref[0] + k, NY), NY)):
            for z, piece in enumerate(pieces):
                rows = piece.shape[1]
                start = (half * ZH + z) * rows
                out_ref[start : start + rows, :] = piece[head]


def join_keys_kernel(*refs):
    pieces, out_refs = refs[:NY], refs[NY:]
    rows = pieces[0].shape[0] // 2
    for half, out_ref in enumerate(out_refs):
        for k, piece in enumerate(pieces):
            out_ref[k * rows : (k + 1) * rows, :] = piece[half * rows : (half + 1) * rows, :]


def attend(both, key_refs, state):
    query = both[:, HD:]
    for ref in key_refs:
        keys = ref[:, : 2 * HD]
        values = ref[:, 2 * HD :]
        scores = lax.dot_general(query, keys[:, :HD], NT, preferred_element_type=F32)
        tangent = lax.dot_general(both, keys, NT, preferred_element_type=F32)
        top = jnp.max(scores, axis=1, keepdims=True)
        if state is None:
            peak = jnp.broadcast_to(top, (scores.shape[0], HD))
        else:
            peak_old, total, total_tan, numer, numer_tan = state
            peak = jnp.maximum(peak_old, top)
            fade = jnp.exp2((peak_old - peak) * EXP2_SCALE)
        expo = jnp.exp2((scores - peak[:, :1]) * EXP2_SCALE)
        expo_tan = expo * tangent
        cuts = range(0, scores.shape[1], HD)
        add = sum(expo[:, c : c + HD] for c in cuts)
        add_tan = sum(expo_tan[:, c : c + HD] for c in cuts)
        pair = jnp.dot(expo.astype(BF16), values, preferred_element_type=F32)
        single = jnp.dot(expo_tan.astype(BF16), values[:, :HD], preferred_element_type=F32)
        if state is None:
            state = (peak, add, add_tan, pair, single)
        else:
            state = (
                peak,
                total * fade + add,
                total_tan * fade + add_tan,
                numer * jnp.concatenate([fade, fade], axis=1) + pair,
                numer_tan * fade + single,
            )
    return state


def finish(state):
    _, total, total_tan, numer, numer_tan = state
    inverse = 1.0 / jnp.sum(total, axis=1, keepdims=True)
    total_tan = jnp.sum(total_tan, axis=1, keepdims=True) * SCALE
    attended = numer[:, :HD] * inverse
    attended_tan = (numer_tan * SCALE + numer[:, HD:] - attended * total_tan) * inverse
    return jnp.concatenate([attended, attended_tan], axis=0).astype(BF16)


def load_state(ref, tile):
    cut = [ref[tile, :, c * HD : (c + 1) * HD] for c in range(3)]
    return (*cut, ref[tile, :, 3 * HD : 5 * HD], ref[tile, :, 5 * HD :])


def attend_kernel(tiles, first, joined, *refs):
    queries, refs = refs[: len(tiles)], refs[len(tiles) :]
    (shared, own), refs = refs[:2], refs[2:]
    if not first:
        state_in, refs = refs[0], refs[1:]
    for place, tile in enumerate(tiles):
        state = None if first else load_state(state_in, tile)
        state = attend(queries[place][...], [shared if tile < NY else own], state)
        if joined is None:
            refs[0][tile] = jnp.concatenate(state, axis=1)
        elif joined:
            refs[0][:, place * HD : (place + 1) * HD] = finish(state)
        else:
            refs[place][...] = finish(state)


def attend_step(blocks, shared, own, state, tiles=tuple(range(NY + 1)), joined=None):
    rows = blocks[0].shape[0]
    if joined is None:
        outs = [jax.ShapeDtypeStruct((NY + 1, rows, 6 * HD), F32)]
    elif joined:
        outs = [jax.ShapeDtypeStruct((2 * rows, len(tiles) * HD), BF16)]
    else:
        outs = [jax.ShapeDtypeStruct((2 * rows, HD), BF16)] * len(tiles)
    carried = [] if state is None else [state]
    found = call(
        functools.partial(attend_kernel, tiles, state is None, joined),
        outs,
        *[blocks[tile] for tile in tiles],
        shared,
        own,
        *carried,
        flops=len(tiles) * rows * shared.shape[0] * 1792,
    )
    return found if joined is False else found[0]


def cut_weight_kernel(y_ref, place_ref, w_ref, *refs):
    out_refs, sems = refs[:-1], refs[-1]
    columns = out_refs[0].shape[1]
    copies = []
    for flip, out_ref in enumerate(out_refs):
        block = lax.bitwise_xor(place_ref[0], flip)
        lanes = pl.ds(pl.multiple_of(block * columns, HD), columns)
        for slot, k in enumerate(SLOTS):
            head = lax.rem(y_ref[0] + k, NY) if k < NY else NY
            source = w_ref.at[pl.ds(pl.multiple_of(head * HD, HD), HD), lanes]
            target = out_ref.at[slot * HD : (slot + 1) * HD]
            copies.append(pltpu.make_async_copy(source, target, sems.at[flip, slot]))
    for copy in copies:
        copy.start()
    for copy in copies:
        copy.wait()


def project_first_kernel(*refs):
    weights, out_ref = refs[6:10], refs[10]
    own, far_rows = 2 * HD, 5 * HD
    total = None
    for ref, weight, low, high in (
        (refs[0], weights[0], 0, own),
        (refs[1], weights[0], own, far_rows),
        (refs[2], weights[1], 0, own),
        (refs[3], weights[1], own, far_rows),
        (refs[4], weights[2], 0, own),
        (refs[5], weights[3], 0, own),
    ):
        part = jnp.dot(ref[...], weight[low:high, :], preferred_element_type=F32)
        total = part if total is None else total + part
    out_ref[...] = total


def project_last_kernel(a_ref, b_ref, w_ref, u_ref, sum_ref, out_ref, tan_ref):
    rows, tile = out_ref.shape
    depth = a_ref.shape[1]
    lanes = pl.ds(pl.multiple_of(pl.program_id(0) * tile, tile), tile)
    weights = pl.ds(w_ref.shape[0] - depth, depth)
    for ref, half in ((out_ref, pl.ds(0, rows)), (tan_ref, pl.ds(rows, rows))):
        total = (
            sum_ref[half, lanes]
            + jnp.dot(a_ref[half, :], w_ref[weights, lanes], preferred_element_type=F32)
            + jnp.dot(b_ref[half, :], u_ref[weights, lanes], preferred_element_type=F32)
        )
        ref[...] = total.astype(BF16)


def project_last(near, far, weight_near, weight_far, partial):
    rows, columns = partial.shape
    tile = 256
    half = pl.BlockSpec((rows // 2, tile), lambda j: (0, j))
    return pl.pallas_call(
        project_last_kernel,
        grid=(columns // tile,),
        in_specs=[VMEM] * 5,
        out_specs=[half, half],
        out_shape=[jax.ShapeDtypeStruct((rows // 2, columns), BF16)] * 2,
        name="project_last",
        compiler_params=pltpu.CompilerParams(vmem_limit_bytes=16 << 20),
    )(near, far, weight_near, weight_far, partial)


def shard_step(queries, keys, values, query_tan, key_tan, value_tan, out_weight):
    rows, width = queries.shape
    heads = width // HD
    slab = keys.shape[0]
    columns = out_weight.shape[1] // (ZL * CORES)
    place = lax.axis_index("head").astype(jnp.int32).reshape(1)
    tok = lax.axis_index("tok").astype(jnp.int32).reshape(1)
    y = jnp.where(place % CORES == 0, tok % NY, tok // NY % NX)
    with_index = [SMEM] + [VMEM] * 8
    out_weight = pltpu.with_memory_space_constraint(out_weight, pltpu.HBM)
    keys, values, query_tan, key_tan, value_tan, queries = (
        pltpu.with_memory_space_constraint(array, pltpu.HBM)
        for array in (keys, values, query_tan, key_tan, value_tan, queries)
    )

    packed = call(
        pack_keys_kernel,
        jax.ShapeDtypeStruct((heads, slab, 4 * HD), BF16),
        keys,
        key_tan,
        values,
        value_tan,
        specs=[HBM] * 4,
        scratch_shapes=[pltpu.VMEM((4, slab, width), BF16), pltpu.SemaphoreType.DMA((4,))],
    )
    pieces = [packed] + [shift(packed, zh=k) for k in (1, 3, 2)]

    sends = call(
        pack_queries_kernel,
        [jax.ShapeDtypeStruct((rows, 2 * HD), BF16)] * (NY + 1),
        y,
        queries,
        query_tan,
        specs=[SMEM, HBM, HBM],
        scratch_shapes=[pltpu.VMEM((2, rows, width), BF16), pltpu.SemaphoreType.DMA((2,))],
    )
    blocks = [sends[0]] + [shift(sends[k], swap=k) for k in (1, 2, 3)] + [sends[NY]]

    place, _ = lax.optimization_barrier((place, sends[1]))
    cuts = call(
        cut_weight_kernel,
        [jax.ShapeDtypeStruct((width, columns), BF16)] * (ZL * CORES),
        y,
        place,
        out_weight,
        specs=[SMEM, SMEM, HBM],
        scratch_shapes=[pltpu.SemaphoreType.DMA((ZL * CORES, NY + 1))],
    )
    pieces, cuts = lax.optimization_barrier((pieces, cuts))

    split = call(
        split_keys_kernel,
        [jax.ShapeDtypeStruct((2 * ZH * slab, 4 * HD), BF16)] * NY,
        y,
        *pieces,
        specs=with_index[: ZH + 1],
    )
    cuts, _ = lax.optimization_barrier((cuts, split[0]))
    weight_near = shift(cuts[2], zl=1)
    weight_far = across(cuts[3])
    weight_core = shift(cuts[1], core=1)

    own = call(
        join_keys_kernel,
        [jax.ShapeDtypeStruct((NY * ZH * slab, 4 * HD), BF16)] * 2,
        split[0],
        *[shift(split[k], swap=k) for k in (1, 3, 2)],
    )
    left = [shift(own[0], ring=1), shift(own[1], ring=1)]
    right = [shift(own[0], ring=-1), shift(own[1], ring=-1)]
    opposite = [shift(left[0], ring=1), shift(right[1], ring=-1)]

    state = attend_step(blocks, own[0], own[1], None)
    state = attend_step(blocks, left[0], right[1], state)
    state = attend_step(blocks, right[0], left[1], state)
    others = attend_step(blocks, opposite[0], opposite[1], state, (1, 2, 3), False)
    opposite[1], _ = lax.optimization_barrier((opposite[1], others[0]))
    mine = [attend_step(blocks, opposite[0], opposite[1], state, (0, NY), True)]
    back = [shift(others[k - 1], swap=-k) for k in (1, 2, 3)]
    mine.append(jnp.concatenate(back, axis=1))

    near = [shift(mine[n], zl=1) for n in range(2)]
    sibling = [shift(mine[n], core=1) for n in range(2)]
    far = shift(near[0], core=1)
    partial = call(
        project_first_kernel,
        jax.ShapeDtypeStruct((2 * rows, columns), F32),
        *mine,
        *sibling,
        near[0],
        far,
        cuts[0],
        weight_core,
        weight_near,
        weight_far,
        flops=10 * rows * width * columns,
    )
    last, partial = lax.optimization_barrier((near[1], partial))
    far = shift(last, core=1)
    return tuple(project_last(last, far, weight_near, weight_far, partial))


def solution(mesh):
    spec = P("tok", "head")
    return jax.shard_map(
        shard_step,
        mesh=mesh,
        in_specs=(spec,) * 6 + (P("head", None),),
        out_specs=(spec, spec),
        check_vma=False,
    )
```

```python
import functools

import jax
import jax.numpy as jnp
from jax import lax
from jax.experimental import pallas as pl
from jax.experimental.pallas import tpu as pltpu
from jax.sharding import PartitionSpec as P


HD = 128
SCALE = HD**-0.5
EXP2_SCALE = SCALE * 1.4426950408889634
NT = (((1,), (1,)), ((), ()))
ZH, NX, NY, ZL, CORES = 4, 4, 4, 2, 2
SLOTS = (0, NY, 1, 2, 3)
AXES = ("tok", "head")


VMEM = pl.BlockSpec(memory_space=pltpu.VMEM)
SMEM = pl.BlockSpec(memory_space=pltpu.SMEM)
HBM = pl.BlockSpec(memory_space=pltpu.HBM)
BF16 = jnp.bfloat16
F32 = jnp.float32


def shift(array, zh=0, swap=0, ring=0, zl=0, core=0):
    pairs = []
    for index in range(ZH * NX * NY * ZL * CORES):
        rest, c = divmod(index, CORES)
        rest, b = divmod(rest, ZL)
        rest, j = divmod(rest, NY)
        a, i = divmod(rest, NX)
        x, y = (swap, ring) if c else (ring, swap)
        to = ((a + zh) % ZH, (i + x) % NX, (j + y) % NY, (b + zl) % ZL, (c + core) % CORES)
        target = (((to[0] * NX + to[1]) * NY + to[2]) * ZL + to[3]) * CORES + to[4]
        pairs.append((index, target))
    return lax.ppermute(array, AXES, pairs)


def across(array):
    pairs = []
    for index in range(ZH * NX * NY * ZL * CORES):
        rest, c = divmod(index, CORES)
        rest, b = divmod(rest, ZL)
        a, xy = divmod(rest, NX * NY)
        to = (a + 1) % ZH if b else (a - 1) % ZH
        pairs.append((index, ((to * NX * NY + xy) * ZL + 1 - b) * CORES + 1 - c))
    return lax.ppermute(array, AXES, pairs)


def call(kernel, outs, *operands, flops=0, specs=None, limit=16, **kwargs):
    return called(kernel, outs, operands, flops, specs, limit, kwargs)


def called(kernel, outs, operands, flops, specs, limit, kwargs):
    return pl.pallas_call(
        kernel,
        out_shape=outs,
        in_specs=specs or [VMEM] * len(operands),
        out_specs=jax.tree.map(lambda _: VMEM, outs),
        compiler_params=pltpu.CompilerParams(vmem_limit_bytes=limit << 20),
        cost_estimate=pl.CostEstimate(
            flops=flops,
            transcendentals=0,
            bytes_accessed=sum(o.size * o.dtype.itemsize for o in operands),
        ),
        **kwargs,
    )(*operands)


def fetch(source_refs, held_ref, sems):
    copies = [
        pltpu.make_async_copy(ref, held_ref.at[slot], sems.at[slot]) for slot, ref in enumerate(source_refs)
    ]
    for copy in copies:
        copy.start()
    for copy in copies:
        copy.wait()


def pack_keys_kernel(k_ref, dk_ref, v_ref, dv_ref, out_ref, held_ref, sems):
    fetch((k_ref, dk_ref, v_ref, dv_ref), held_ref, sems)
    for head in range(out_ref.shape[0]):
        for slot in range(4):
            out_ref[head, :, slot * HD : (slot + 1) * HD] = held_ref[slot, :, head * HD : (head + 1) * HD]


def pack_queries_kernel(y_ref, q_ref, dq_ref, *refs):
    out_refs, (held_ref, sems) = refs[:-2], refs[-2:]
    fetch((dq_ref, q_ref), held_ref, sems)
    for k, out_ref in enumerate(out_refs):
        head = lax.rem(y_ref[0] + k, NY) if k < NY else NY
        lanes = pl.ds(pl.multiple_of(head * HD, HD), HD)
        out_ref[:, :HD] = held_ref[0, :, lanes]
        out_ref[:, HD:] = held_ref[1, :, lanes]


def split_keys_kernel(y_ref, *refs):
    pieces, out_refs = refs[:ZH], refs[ZH:]
    for k, out_ref in enumerate(out_refs):
        for half, head in enumerate((lax.rem(y_ref[0] + k, NY), NY)):
            for z, piece in enumerate(pieces):
                rows = piece.shape[1]
                start = (half * ZH + z) * rows
                out_ref[start : start + rows, :] = piece[head]


def join_keys_kernel(*refs):
    pieces, out_refs = refs[:NY], refs[NY:]
    rows = pieces[0].shape[0] // 2
    for half, out_ref in enumerate(out_refs):
        for k, piece in enumerate(pieces):
            out_ref[k * rows : (k + 1) * rows, :] = piece[half * rows : (half + 1) * rows, :]


def attend(both, key_refs, state):
    query = both[:, HD:]
    for ref in key_refs:
        keys = ref[:, : 2 * HD]
        values = ref[:, 2 * HD :]
        scores = lax.dot_general(query, keys[:, :HD], NT, preferred_element_type=F32)
        tangent = lax.dot_general(both, keys, NT, preferred_element_type=F32)
        top = jnp.max(scores, axis=1, keepdims=True)
        if state is None:
            peak = jnp.broadcast_to(top, (scores.shape[0], HD))
        else:
            peak_old, total, total_tan, numer, numer_tan = state
            peak = jnp.maximum(peak_old, top)
            fade = jnp.exp2((peak_old - peak) * EXP2_SCALE)
        expo = jnp.exp2((scores - peak[:, :1]) * EXP2_SCALE)
        expo_tan = expo * tangent
        cuts = range(0, scores.shape[1], HD)
        add = sum(expo[:, c : c + HD] for c in cuts)
        add_tan = sum(expo_tan[:, c : c + HD] for c in cuts)
        pair = jnp.dot(expo.astype(BF16), values, preferred_element_type=F32)
        single = jnp.dot(expo_tan.astype(BF16), values[:, :HD], preferred_element_type=F32)
        if state is None:
            state = (peak, add, add_tan, pair, single)
        else:
            state = (
                peak,
                total * fade + add,
                total_tan * fade + add_tan,
                numer * jnp.concatenate([fade, fade], axis=1) + pair,
                numer_tan * fade + single,
            )
    return state


def finish(state):
    _, total, total_tan, numer, numer_tan = state
    inverse = 1.0 / jnp.sum(total, axis=1, keepdims=True)
    total_tan = jnp.sum(total_tan, axis=1, keepdims=True) * SCALE
    attended = numer[:, :HD] * inverse
    attended_tan = (numer_tan * SCALE + numer[:, HD:] - attended * total_tan) * inverse
    return jnp.concatenate([attended, attended_tan], axis=0).astype(BF16)


def load_state(ref, tile):
    cut = [ref[tile, :, c * HD : (c + 1) * HD] for c in range(3)]
    return (*cut, ref[tile, :, 3 * HD : 5 * HD], ref[tile, :, 5 * HD :])


def attend_kernel(tiles, first, joined, *refs):
    queries, refs = refs[: len(tiles)], refs[len(tiles) :]
    (shared, own), refs = refs[:2], refs[2:]
    if not first:
        state_in, refs = refs[0], refs[1:]
    for place, tile in enumerate(tiles):
        state = None if first else load_state(state_in, tile)
        state = attend(queries[place][...], [shared if tile < NY else own], state)
        if joined is None:
            refs[0][tile] = jnp.concatenate(state, axis=1)
        elif joined:
            refs[0][:, place * HD : (place + 1) * HD] = finish(state)
        else:
            done = finish(state)
            refs[place][...] = done
            refs[-1][:, place * HD : (place + 1) * HD] = done


def attend_step(blocks, shared, own, state, tiles=tuple(range(NY + 1)), joined=None):
    rows = blocks[0].shape[0]
    if joined is None:
        outs = [jax.ShapeDtypeStruct((NY + 1, rows, 6 * HD), F32)]
    elif joined:
        outs = [jax.ShapeDtypeStruct((2 * rows, len(tiles) * HD), BF16)]
    else:
        outs = [jax.ShapeDtypeStruct((2 * rows, HD), BF16)] * len(tiles)
        outs.append(jax.ShapeDtypeStruct((2 * rows, len(tiles) * HD), BF16))
    carried = [] if state is None else [state]
    found = call(
        functools.partial(attend_kernel, tiles, state is None, joined),
        outs,
        *[blocks[tile] for tile in tiles],
        shared,
        own,
        *carried,
        flops=len(tiles) * rows * shared.shape[0] * 1792,
    )
    return found if joined is False else found[0]


def cut_weight_kernel(y_ref, place_ref, w_ref, *refs):
    out_refs, sems = refs[:-1], refs[-1]
    columns = out_refs[0].shape[1]
    copies = []
    for flip, out_ref in enumerate(out_refs):
        block = lax.bitwise_xor(place_ref[0], flip)
        lanes = pl.ds(pl.multiple_of(block * columns, HD), columns)
        for slot, k in enumerate(SLOTS):
            head = lax.rem(y_ref[0] + k, NY) if k < NY else NY
            source = w_ref.at[pl.ds(pl.multiple_of(head * HD, HD), HD), lanes]
            target = out_ref.at[slot * HD : (slot + 1) * HD]
            copies.append(pltpu.make_async_copy(source, target, sems.at[flip, slot]))
    for copy in copies:
        copy.start()
    for copy in copies:
        copy.wait()


def project_sum(refs, weights, lanes=slice(None)):
    own = refs[0].shape[1]
    total = None
    for place, ref in enumerate(refs):
        start = own * (place % 2)
        rows = slice(start, start + ref.shape[1])
        part = jnp.dot(ref[...], weights[place // 2][rows, lanes], preferred_element_type=F32)
        total = part if total is None else total + part
    return total


def project_first_kernel(*refs):
    refs[6][...] = project_sum(refs[:4], refs[4:6])


def project_last_kernel(*refs):
    sum_ref, out_ref, tan_ref = refs[6:]
    rows, tile = out_ref.shape
    lanes = pl.ds(pl.multiple_of(pl.program_id(0) * tile, tile), tile)
    total = sum_ref[:, lanes] + project_sum(refs[:4], refs[4:6], lanes)
    out_ref[...] = total[:rows].astype(BF16)
    tan_ref[...] = total[rows:].astype(BF16)


def project_last(*operands):
    rows, columns = operands[-1].shape
    tile = 256
    half = pl.BlockSpec((rows // 2, tile), lambda j: (0, j))
    return pl.pallas_call(
        project_last_kernel,
        grid=(columns // tile,),
        in_specs=[VMEM] * len(operands),
        out_specs=[half, half],
        out_shape=[jax.ShapeDtypeStruct((rows // 2, columns), BF16)] * 2,
        name="project_last",
        compiler_params=pltpu.CompilerParams(vmem_limit_bytes=16 << 20),
    )(*operands)


def shard_step(queries, keys, values, query_tan, key_tan, value_tan, out_weight):
    rows, width = queries.shape
    heads = width // HD
    slab = keys.shape[0]
    columns = out_weight.shape[1] // (ZL * CORES)
    place = lax.axis_index("head").astype(jnp.int32).reshape(1)
    tok = lax.axis_index("tok").astype(jnp.int32).reshape(1)
    y = jnp.where(place % CORES == 0, tok % NY, tok // NY % NX)
    with_index = [SMEM] + [VMEM] * 8
    out_weight = pltpu.with_memory_space_constraint(out_weight, pltpu.HBM)
    keys, values, query_tan, key_tan, value_tan, queries = (
        pltpu.with_memory_space_constraint(array, pltpu.HBM)
        for array in (keys, values, query_tan, key_tan, value_tan, queries)
    )

    packed = call(
        pack_keys_kernel,
        jax.ShapeDtypeStruct((heads, slab, 4 * HD), BF16),
        keys,
        key_tan,
        values,
        value_tan,
        specs=[HBM] * 4,
        scratch_shapes=[pltpu.VMEM((4, slab, width), BF16), pltpu.SemaphoreType.DMA((4,))],
    )
    pieces = [packed] + [shift(packed, zh=k) for k in (1, 3, 2)]

    sends = call(
        pack_queries_kernel,
        [jax.ShapeDtypeStruct((rows, 2 * HD), BF16)] * (NY + 1),
        y,
        queries,
        query_tan,
        specs=[SMEM, HBM, HBM],
        scratch_shapes=[pltpu.VMEM((2, rows, width), BF16), pltpu.SemaphoreType.DMA((2,))],
    )
    blocks = [sends[0]] + [shift(sends[k], swap=k) for k in (1, 2, 3)] + [sends[NY]]

    place, _ = lax.optimization_barrier((place, sends[1]))
    cuts = call(
        cut_weight_kernel,
        [jax.ShapeDtypeStruct((width, columns), BF16)] * (ZL * CORES),
        y,
        place,
        out_weight,
        specs=[SMEM, SMEM, HBM],
        scratch_shapes=[pltpu.SemaphoreType.DMA((ZL * CORES, NY + 1))],
    )
    pieces, cuts = lax.optimization_barrier((pieces, cuts))

    split = call(
        split_keys_kernel,
        [jax.ShapeDtypeStruct((2 * ZH * slab, 4 * HD), BF16)] * NY,
        y,
        *pieces,
        specs=with_index[: ZH + 1],
    )
    cuts, _ = lax.optimization_barrier((cuts, split[0]))
    weight_near = shift(cuts[2], zl=1)
    weight_far = across(cuts[3])
    weight_core = shift(cuts[1], core=1)

    own = call(
        join_keys_kernel,
        [jax.ShapeDtypeStruct((NY * ZH * slab, 4 * HD), BF16)] * 2,
        split[0],
        *[shift(split[k], swap=k) for k in (1, 3, 2)],
    )
    left = [shift(own[0], ring=1), shift(own[1], ring=1)]
    right = [shift(own[0], ring=-1), shift(own[1], ring=-1)]
    opposite = [shift(left[0], ring=1), shift(right[1], ring=-1)]

    state = attend_step(blocks, own[0], own[1], None)
    state = attend_step(blocks, left[0], right[1], state)
    state = attend_step(blocks, right[0], left[1], state)
    others = attend_step(blocks, opposite[0], opposite[0], state, (1, 2, 3), False)
    opposite[1], _ = lax.optimization_barrier((opposite[1], others[0]))
    mine = [attend_step(blocks, opposite[0], opposite[1], state, (0, NY), True)]
    back = [shift(others[k - 1], swap=-k) for k in (1, 2, 3)]
    mine.append(jnp.concatenate(back, axis=1))

    sibling = [shift(mine[n], core=1) for n in range(2)]
    partial = call(
        project_first_kernel,
        jax.ShapeDtypeStruct((2 * rows, columns), F32),
        *mine,
        *sibling,
        cuts[0],
        weight_core,
        flops=8 * rows * width * columns,
    )

    crossed = shift(others[NY - 1], zl=1)
    handed = [shift(crossed[:, (k - 1) * HD : k * HD], swap=-k) for k in (1, 2, 3)]
    near = [shift(mine[0], zl=1), jnp.concatenate(handed, axis=1)]
    far = [shift(near[n], core=1) for n in range(2)]
    return tuple(project_last(*near, *far, weight_near, weight_far, partial))


def solution(mesh):
    spec = P("tok", "head")
    return jax.shard_map(
        shard_step,
        mesh=mesh,
        in_specs=(spec,) * 6 + (P("head", None),),
        out_specs=(spec, spec),
        check_vma=False,
    )
```

```python
import functools

import jax
import jax.numpy as jnp
from jax import lax
from jax.experimental import pallas as pl
from jax.experimental.pallas import tpu as pltpu
from jax.sharding import PartitionSpec as P


HD = 128
SCALE = HD**-0.5
EXP2_SCALE = SCALE * 1.4426950408889634
NT = (((1,), (1,)), ((), ()))
ZH, NX, NY, ZL, CORES = 4, 4, 4, 2, 2
SLOTS = (0, NY, 1, 2, 3)
AXES = ("tok", "head")


VMEM = pl.BlockSpec(memory_space=pltpu.VMEM)
SMEM = pl.BlockSpec(memory_space=pltpu.SMEM)
HBM = pl.BlockSpec(memory_space=pltpu.HBM)
BF16 = jnp.bfloat16
F32 = jnp.float32


def shift(array, zh=0, swap=0, ring=0, zl=0, core=0):
    pairs = []
    for index in range(ZH * NX * NY * ZL * CORES):
        rest, c = divmod(index, CORES)
        rest, b = divmod(rest, ZL)
        rest, j = divmod(rest, NY)
        a, i = divmod(rest, NX)
        x, y = (swap, ring) if c else (ring, swap)
        to = ((a + zh) % ZH, (i + x) % NX, (j + y) % NY, (b + zl) % ZL, (c + core) % CORES)
        target = (((to[0] * NX + to[1]) * NY + to[2]) * ZL + to[3]) * CORES + to[4]
        pairs.append((index, target))
    return lax.ppermute(array, AXES, pairs)


def across(array, core=0):
    pairs = []
    for index in range(ZH * NX * NY * ZL * CORES):
        rest, c = divmod(index, CORES)
        rest, b = divmod(rest, ZL)
        a, xy = divmod(rest, NX * NY)
        to = (a + 1) % ZH if b else (a - 1) % ZH
        pairs.append((index, ((to * NX * NY + xy) * ZL + 1 - b) * CORES + (c + core) % CORES))
    return lax.ppermute(array, AXES, pairs)


def call(kernel, outs, *operands, flops=0, specs=None, limit=16, **kwargs):
    return called(kernel, outs, operands, flops, specs, limit, kwargs)


def called(kernel, outs, operands, flops, specs, limit, kwargs):
    return pl.pallas_call(
        kernel,
        out_shape=outs,
        in_specs=specs or [VMEM] * len(operands),
        out_specs=jax.tree.map(lambda _: VMEM, outs),
        compiler_params=pltpu.CompilerParams(vmem_limit_bytes=limit << 20),
        cost_estimate=pl.CostEstimate(
            flops=flops,
            transcendentals=0,
            bytes_accessed=sum(o.size * o.dtype.itemsize for o in operands),
        ),
        **kwargs,
    )(*operands)


def fetch(source_refs, held_ref, sems):
    copies = [
        pltpu.make_async_copy(ref, held_ref.at[slot], sems.at[slot]) for slot, ref in enumerate(source_refs)
    ]
    for copy in copies:
        copy.start()
    for copy in copies:
        copy.wait()


def pack_keys_kernel(k_ref, dk_ref, v_ref, dv_ref, out_ref, held_ref, sems):
    fetch((k_ref, dk_ref, v_ref, dv_ref), held_ref, sems)
    for head in range(out_ref.shape[0]):
        for slot in range(4):
            out_ref[head, :, slot * HD : (slot + 1) * HD] = held_ref[slot, :, head * HD : (head + 1) * HD]


def pack_queries_kernel(y_ref, q_ref, dq_ref, *refs):
    out_refs, (held_ref, sems) = refs[:-2], refs[-2:]
    fetch((dq_ref, q_ref), held_ref, sems)
    for k, out_ref in enumerate(out_refs):
        head = lax.rem(y_ref[0] + k, NY) if k < NY else NY
        lanes = pl.ds(pl.multiple_of(head * HD, HD), HD)
        out_ref[:, :HD] = held_ref[0, :, lanes]
        out_ref[:, HD:] = held_ref[1, :, lanes]


def split_keys_kernel(y_ref, *refs):
    pieces, out_refs = refs[:ZH], refs[ZH:]
    for k, out_ref in enumerate(out_refs):
        for half, head in enumerate((lax.rem(y_ref[0] + k, NY), NY)):
            for z, piece in enumerate(pieces):
                rows = piece.shape[1]
                start = (half * ZH + z) * rows
                out_ref[start : start + rows, :] = piece[head]


def join_keys_kernel(*refs):
    pieces, out_refs = refs[:NY], refs[NY:]
    rows = pieces[0].shape[0] // 2
    for half, out_ref in enumerate(out_refs):
        for k, piece in enumerate(pieces):
            out_ref[k * rows : (k + 1) * rows, :] = piece[half * rows : (half + 1) * rows, :]


def attend(both, key_refs, state):
    query = both[:, HD:]
    for ref in key_refs:
        keys = ref[:, : 2 * HD]
        values = ref[:, 2 * HD :]
        scores = lax.dot_general(query, keys[:, :HD], NT, preferred_element_type=F32)
        tangent = lax.dot_general(both, keys, NT, preferred_element_type=F32)
        top = jnp.max(scores, axis=1, keepdims=True)
        if state is None:
            peak = jnp.broadcast_to(top, (scores.shape[0], HD))
        else:
            peak_old, total, total_tan, numer, numer_tan = state
            peak = jnp.maximum(peak_old, top)
            fade = jnp.exp2((peak_old - peak) * EXP2_SCALE)
        expo = jnp.exp2((scores - peak[:, :1]) * EXP2_SCALE)
        expo_tan = expo * tangent
        cuts = range(0, scores.shape[1], HD)
        add = sum(expo[:, c : c + HD] for c in cuts)
        add_tan = sum(expo_tan[:, c : c + HD] for c in cuts)
        pair = jnp.dot(expo.astype(BF16), values, preferred_element_type=F32)
        single = jnp.dot(expo_tan.astype(BF16), values[:, :HD], preferred_element_type=F32)
        if state is None:
            state = (peak, add, add_tan, pair, single)
        else:
            state = (
                peak,
                total * fade + add,
                total_tan * fade + add_tan,
                numer * jnp.concatenate([fade, fade], axis=1) + pair,
                numer_tan * fade + single,
            )
    return state


def finish(state):
    _, total, total_tan, numer, numer_tan = state
    inverse = 1.0 / jnp.sum(total, axis=1, keepdims=True)
    total_tan = jnp.sum(total_tan, axis=1, keepdims=True) * SCALE
    attended = numer[:, :HD] * inverse
    attended_tan = (numer_tan * SCALE + numer[:, HD:] - attended * total_tan) * inverse
    return jnp.concatenate([attended, attended_tan], axis=0).astype(BF16)


def load_state(ref, tile):
    cut = [ref[tile, :, c * HD : (c + 1) * HD] for c in range(3)]
    return (*cut, ref[tile, :, 3 * HD : 5 * HD], ref[tile, :, 5 * HD :])


def attend_kernel(tiles, first, joined, *refs):
    queries, refs = refs[: len(tiles)], refs[len(tiles) :]
    (shared, own), refs = refs[:2], refs[2:]
    if not first:
        state_in, refs = refs[0], refs[1:]
    for place, tile in enumerate(tiles):
        state = None if first else load_state(state_in, tile)
        state = attend(queries[place][...], [shared if tile < NY else own], state)
        if joined is None:
            refs[0][tile] = jnp.concatenate(state, axis=1)
        elif joined:
            refs[0][:, place * HD : (place + 1) * HD] = finish(state)
        else:
            refs[place][...] = finish(state)


def attend_step(blocks, shared, own, state, tiles=tuple(range(NY + 1)), joined=None):
    rows = blocks[0].shape[0]
    if joined is None:
        outs = [jax.ShapeDtypeStruct((NY + 1, rows, 6 * HD), F32)]
    elif joined:
        outs = [jax.ShapeDtypeStruct((2 * rows, len(tiles) * HD), BF16)]
    else:
        outs = [jax.ShapeDtypeStruct((2 * rows, HD), BF16)] * len(tiles)
    carried = [] if state is None else [state]
    found = call(
        functools.partial(attend_kernel, tiles, state is None, joined),
        outs,
        *[blocks[tile] for tile in tiles],
        shared,
        own,
        *carried,
        flops=len(tiles) * rows * shared.shape[0] * 1792,
    )
    return found if joined is False else found[0]


def cut_weight_kernel(y_ref, place_ref, w_ref, *refs):
    out_refs, sems = refs[:-1], refs[-1]
    columns = out_refs[0].shape[1]
    copies = []
    for flip in range(ZL * CORES):
        block = lax.bitwise_xor(place_ref[0], flip)
        lanes = pl.ds(pl.multiple_of(block * columns, HD), columns)
        for slot, k in enumerate(SLOTS):
            head = lax.rem(y_ref[0] + k, NY) if k < NY else NY
            source = w_ref.at[pl.ds(pl.multiple_of(head * HD, HD), HD), lanes]
            if flip == ZL and slot == NY:
                target = out_refs[-1]
            else:
                target = out_refs[flip].at[slot * HD : (slot + 1) * HD]
            copies.append(pltpu.make_async_copy(source, target, sems.at[flip, slot]))
    for copy in copies:
        copy.start()
    for copy in copies:
        copy.wait()


def project_sum(pairs, lanes=slice(None)):
    total = None
    for ref, columns, weight, row in pairs:
        low, high = columns
        rows = slice(row, row + high - low)
        part = jnp.dot(ref[:, low:high], weight[rows, lanes], preferred_element_type=F32)
        total = part if total is None else total + part
    return total


OWN, REST, MOST = (0, 2 * HD), (0, 3 * HD), (0, 2 * HD)


def project_first_kernel(a_ref, b_ref, c_ref, d_ref, wa_ref, wb_ref, wc_ref, wm_ref, wd_ref, out_ref):
    out_ref[...] = project_sum(
        (
            (a_ref, OWN, wa_ref, 0),
            (b_ref, OWN, wb_ref, 0),
            (c_ref, MOST, wc_ref, 2 * HD),
            (c_ref, (2 * HD, 3 * HD), wm_ref, 0),
            (d_ref, REST, wd_ref, 2 * HD),
        )
    )


def project_last_kernel(a_ref, b_ref, c_ref, d_ref, wa_ref, wb_ref, wc_ref, wd_ref, sum_ref, out_ref, tan_ref):
    rows, tile = out_ref.shape
    lanes = pl.ds(pl.multiple_of(pl.program_id(0) * tile, tile), tile)
    total = sum_ref[:, lanes] + project_sum(
        (
            (a_ref, REST, wa_ref, 2 * HD),
            (b_ref, REST, wb_ref, 2 * HD),
            (c_ref, OWN, wc_ref, 0),
            (d_ref, OWN, wd_ref, 0),
        ),
        lanes,
    )
    out_ref[...] = total[:rows].astype(BF16)
    tan_ref[...] = total[rows:].astype(BF16)


def project_last(*operands):
    rows, columns = operands[-1].shape
    tile = 256
    half = pl.BlockSpec((rows // 2, tile), lambda j: (0, j))
    return pl.pallas_call(
        project_last_kernel,
        grid=(columns // tile,),
        in_specs=[VMEM] * len(operands),
        out_specs=[half, half],
        out_shape=[jax.ShapeDtypeStruct((rows // 2, columns), BF16)] * 2,
        name="project_last",
        compiler_params=pltpu.CompilerParams(vmem_limit_bytes=16 << 20),
    )(*operands)


def shard_step(queries, keys, values, query_tan, key_tan, value_tan, out_weight):
    rows, width = queries.shape
    heads = width // HD
    slab = keys.shape[0]
    columns = out_weight.shape[1] // (ZL * CORES)
    place = lax.axis_index("head").astype(jnp.int32).reshape(1)
    tok = lax.axis_index("tok").astype(jnp.int32).reshape(1)
    y = jnp.where(place % CORES == 0, tok % NY, tok // NY % NX)
    with_index = [SMEM] + [VMEM] * 8
    out_weight = pltpu.with_memory_space_constraint(out_weight, pltpu.HBM)
    keys, values, query_tan, key_tan, value_tan, queries = (
        pltpu.with_memory_space_constraint(array, pltpu.HBM)
        for array in (keys, values, query_tan, key_tan, value_tan, queries)
    )

    packed = call(
        pack_keys_kernel,
        jax.ShapeDtypeStruct((heads, slab, 4 * HD), BF16),
        keys,
        key_tan,
        values,
        value_tan,
        specs=[HBM] * 4,
        scratch_shapes=[pltpu.VMEM((4, slab, width), BF16), pltpu.SemaphoreType.DMA((4,))],
    )
    pieces = [packed] + [shift(packed, zh=k) for k in (1, 3, 2)]

    sends = call(
        pack_queries_kernel,
        [jax.ShapeDtypeStruct((rows, 2 * HD), BF16)] * (NY + 1),
        y,
        queries,
        query_tan,
        specs=[SMEM, HBM, HBM],
        scratch_shapes=[pltpu.VMEM((2, rows, width), BF16), pltpu.SemaphoreType.DMA((2,))],
    )
    blocks = [sends[0]] + [shift(sends[k], swap=k) for k in (1, 2, 3)] + [sends[NY]]

    place, _ = lax.optimization_barrier((place, sends[1]))
    cuts = call(
        cut_weight_kernel,
        [
            jax.ShapeDtypeStruct((depth, columns), BF16)
            for depth in (width, width, width - HD, width, HD)
        ],
        y,
        place,
        out_weight,
        specs=[SMEM, SMEM, HBM],
        scratch_shapes=[pltpu.SemaphoreType.DMA((ZL * CORES, NY + 1))],
    )
    pieces, cuts = lax.optimization_barrier((pieces, cuts))

    split = call(
        split_keys_kernel,
        [jax.ShapeDtypeStruct((2 * ZH * slab, 4 * HD), BF16)] * NY,
        y,
        *pieces,
        specs=with_index[: ZH + 1],
    )
    cuts, _ = lax.optimization_barrier((cuts, split[0]))
    weight_near = shift(cuts[2], zl=1)
    weight_far = across(cuts[3], core=1)
    weight_more = across(cuts[4])
    weight_core = shift(cuts[1], core=1)

    own = call(
        join_keys_kernel,
        [jax.ShapeDtypeStruct((NY * ZH * slab, 4 * HD), BF16)] * 2,
        split[0],
        *[shift(split[k], swap=k) for k in (1, 3, 2)],
    )
    left = [shift(own[0], ring=1), shift(own[1], ring=1)]
    right = [shift(own[0], ring=-1), shift(own[1], ring=-1)]
    opposite = [shift(left[0], ring=1), shift(right[1], ring=-1)]

    state = attend_step(blocks, own[0], own[1], None)
    state = attend_step(blocks, left[0], right[1], state)
    state = attend_step(blocks, right[0], left[1], state)
    others = attend_step(blocks, opposite[0], opposite[0], state, (1, 2, 3), False)
    opposite[1], _ = lax.optimization_barrier((opposite[1], others[0]))
    kept = attend_step(blocks, opposite[0], opposite[1], state, (0, NY), True)

    near = [
        shift(kept, zl=1),
        jnp.concatenate([shift(others[k - 1], swap=-k, zl=1) for k in (1, 2, 3)], axis=1),
    ]
    mine = [kept, jnp.concatenate([shift(others[k - 1], swap=-k) for k in (1, 2, 3)], axis=1)]
    sibling = [shift(mine[n], core=1) for n in range(2)]
    far = [shift(near[n], core=1) for n in range(2)]
    weights = (cuts[0], weight_core, weight_near)
    partial = call(
        project_first_kernel,
        jax.ShapeDtypeStruct((2 * rows, columns), F32),
        mine[0],
        sibling[0],
        near[1],
        far[1],
        *weights,
        weight_more,
        weight_far,
        flops=8 * rows * width * columns,
    )
    return tuple(
        project_last(mine[1], sibling[1], near[0], far[0], *weights, weight_far, partial)
    )


def solution(mesh):
    spec = P("tok", "head")
    return jax.shard_map(
        shard_step,
        mesh=mesh,
        in_specs=(spec,) * 6 + (P("head", None),),
        out_specs=(spec, spec),
        check_vma=False,
    )
```

```python
import functools

import jax
import jax.numpy as jnp
from jax import lax
from jax.experimental import pallas as pl
from jax.experimental.pallas import tpu as pltpu
from jax.sharding import PartitionSpec as P


HD = 128
SCALE = HD**-0.5
EXP2_SCALE = SCALE * 1.4426950408889634
NT = (((1,), (1,)), ((), ()))
ZH, NX, NY, ZL, CORES = 4, 4, 4, 2, 2
SLOTS = (0, NY, 1, 2, 3)
AXES = ("tok", "head")


VMEM = pl.BlockSpec(memory_space=pltpu.VMEM)
SMEM = pl.BlockSpec(memory_space=pltpu.SMEM)
HBM = pl.BlockSpec(memory_space=pltpu.HBM)
BF16 = jnp.bfloat16
F32 = jnp.float32


def shift(array, zh=0, swap=0, ring=0, zl=0, core=0):
    pairs = []
    for index in range(ZH * NX * NY * ZL * CORES):
        rest, c = divmod(index, CORES)
        rest, b = divmod(rest, ZL)
        rest, j = divmod(rest, NY)
        a, i = divmod(rest, NX)
        x, y = (swap, ring) if c else (ring, swap)
        to = ((a + zh) % ZH, (i + x) % NX, (j + y) % NY, (b + zl) % ZL, (c + core) % CORES)
        target = (((to[0] * NX + to[1]) * NY + to[2]) * ZL + to[3]) * CORES + to[4]
        pairs.append((index, target))
    return lax.ppermute(array, AXES, pairs)


def across(array, core=0):
    pairs = []
    for index in range(ZH * NX * NY * ZL * CORES):
        rest, c = divmod(index, CORES)
        rest, b = divmod(rest, ZL)
        a, xy = divmod(rest, NX * NY)
        to = (a + 1) % ZH if b else (a - 1) % ZH
        pairs.append((index, ((to * NX * NY + xy) * ZL + 1 - b) * CORES + (c + core) % CORES))
    return lax.ppermute(array, AXES, pairs)


def call(kernel, outs, *operands, flops=0, specs=None, limit=16, **kwargs):
    return called(kernel, outs, operands, flops, specs, limit, kwargs)


def called(kernel, outs, operands, flops, specs, limit, kwargs):
    return pl.pallas_call(
        kernel,
        out_shape=outs,
        in_specs=specs or [VMEM] * len(operands),
        out_specs=jax.tree.map(lambda _: VMEM, outs),
        compiler_params=pltpu.CompilerParams(vmem_limit_bytes=limit << 20),
        cost_estimate=pl.CostEstimate(
            flops=flops,
            transcendentals=0,
            bytes_accessed=sum(o.size * o.dtype.itemsize for o in operands),
        ),
        **kwargs,
    )(*operands)


def fetch(source_refs, held_ref, sems):
    copies = [
        pltpu.make_async_copy(ref, held_ref.at[slot], sems.at[slot]) for slot, ref in enumerate(source_refs)
    ]
    for copy in copies:
        copy.start()
    for copy in copies:
        copy.wait()


def pack_keys_kernel(k_ref, dk_ref, v_ref, dv_ref, out_ref, held_ref, sems):
    fetch((k_ref, dk_ref, v_ref, dv_ref), held_ref, sems)
    for head in range(out_ref.shape[0]):
        for slot in range(4):
            out_ref[head, :, slot * HD : (slot + 1) * HD] = held_ref[slot, :, head * HD : (head + 1) * HD]


def pack_queries_kernel(y_ref, q_ref, dq_ref, *refs):
    out_refs, (held_ref, sems) = refs[:-2], refs[-2:]
    fetch((dq_ref, q_ref), held_ref, sems)
    for k, out_ref in enumerate(out_refs):
        head = lax.rem(y_ref[0] + k, NY) if k < NY else NY
        lanes = pl.ds(pl.multiple_of(head * HD, HD), HD)
        out_ref[:, :HD] = held_ref[0, :, lanes]
        out_ref[:, HD:] = held_ref[1, :, lanes]


def split_keys_kernel(y_ref, *refs):
    pieces, out_refs = refs[:ZH], refs[ZH:]
    for k, out_ref in enumerate(out_refs):
        for half, head in enumerate((lax.rem(y_ref[0] + k, NY), NY)):
            for z, piece in enumerate(pieces):
                rows = piece.shape[1]
                start = (half * ZH + z) * rows
                out_ref[start : start + rows, :] = piece[head]


def join_keys_kernel(*refs):
    pieces, out_refs = refs[:NY], refs[NY:]
    rows = pieces[0].shape[0] // 2
    for half, out_ref in enumerate(out_refs):
        for k, piece in enumerate(pieces):
            out_ref[k * rows : (k + 1) * rows, :] = piece[half * rows : (half + 1) * rows, :]


def attend(both, key_ref, state):
    query = both[:, HD:]
    keys = key_ref[:, : 2 * HD]
    values = key_ref[:, 2 * HD :]
    scores = lax.dot_general(query, keys[:, :HD], NT, preferred_element_type=F32)
    tangent = lax.dot_general(both, keys, NT, preferred_element_type=F32)
    top = jnp.max(scores, axis=1, keepdims=True)
    if state is None:
        peak = jnp.broadcast_to(top, (scores.shape[0], HD))
    else:
        peak_old, total, total_tan, numer, numer_tan = state
        peak = jnp.maximum(peak_old, top)
        fade = jnp.exp2((peak_old - peak) * EXP2_SCALE)
    expo = jnp.exp2((scores - peak[:, :1]) * EXP2_SCALE)
    expo_tan = expo * tangent
    cuts = range(0, scores.shape[1], HD)
    add = sum(expo[:, c : c + HD] for c in cuts)
    add_tan = sum(expo_tan[:, c : c + HD] for c in cuts)
    pair = jnp.dot(expo.astype(BF16), values, preferred_element_type=F32)
    single = jnp.dot(expo_tan.astype(BF16), values[:, :HD], preferred_element_type=F32)
    if state is None:
        return peak, add, add_tan, pair, single
    return (
        peak,
        total * fade + add,
        total_tan * fade + add_tan,
        numer * jnp.concatenate([fade, fade], axis=1) + pair,
        numer_tan * fade + single,
    )


def finish(state):
    _, total, total_tan, numer, numer_tan = state
    inverse = 1.0 / jnp.sum(total, axis=1, keepdims=True)
    total_tan = jnp.sum(total_tan, axis=1, keepdims=True) * SCALE
    attended = numer[:, :HD] * inverse
    attended_tan = (numer_tan * SCALE + numer[:, HD:] - attended * total_tan) * inverse
    return attended.astype(BF16), attended_tan.astype(BF16)


def load_state(ref, rows):
    cut = [ref[rows, c * HD : (c + 1) * HD] for c in range(3)]
    return (*cut, ref[rows, 3 * HD : 5 * HD], ref[rows, 5 * HD :])


def attend_kernel(first, shared_ref, own_ref, shared_keys, own_keys, *refs):
    sides = ((shared_ref, shared_keys, refs[-2]), (own_ref, own_keys, refs[-1]))
    for side, (query, keys, out_ref) in enumerate(sides):
        state = None if first else load_state(refs[side], slice(None))
        out_ref[...] = jnp.concatenate(attend(query[...], keys, state), axis=1)


def attend_step(queries, keys, state):
    rows = [query.shape[0] for query in queries]
    return call(
        functools.partial(attend_kernel, not state),
        [jax.ShapeDtypeStruct((n, 6 * HD), F32) for n in rows],
        *queries,
        *keys,
        *state,
        flops=sum(rows) * keys[0].shape[0] * 1792,
    )


def attend_others_kernel(query_ref, keys, state_ref, *out_refs):
    rows = out_refs[0].shape[0] // 2
    most = slice(0, rows * len(out_refs))
    attended, attended_tan = finish(attend(query_ref[most, :], keys, load_state(state_ref, most)))
    for place, ref in enumerate(out_refs):
        ref[:rows, :] = attended[place * rows : (place + 1) * rows]
        ref[rows:, :] = attended_tan[place * rows : (place + 1) * rows]


def attend_kept_kernel(shared_ref, own_ref, shared_keys, own_keys, shared_state, own_state, out_ref):
    rows = own_ref.shape[0]
    start = shared_ref.shape[0] - rows
    sides = (
        (shared_ref, shared_keys, shared_state, slice(start, start + rows)),
        (own_ref, own_keys, own_state, slice(0, rows)),
    )
    for side, (query, keys, state, part) in enumerate(sides):
        lanes = slice(side * HD, (side + 1) * HD)
        attended, attended_tan = finish(attend(query[part, :], keys, load_state(state, part)))
        out_ref[:rows, lanes] = attended
        out_ref[rows:, lanes] = attended_tan


def cut_weight_kernel(y_ref, place_ref, w_ref, *refs):
    out_refs, sems = refs[:-1], refs[-1]
    columns = out_refs[0].shape[1]
    copies = []
    for flip in range(ZL * CORES):
        block = lax.bitwise_xor(place_ref[0], flip)
        lanes = pl.ds(pl.multiple_of(block * columns, HD), columns)
        for slot, k in enumerate(SLOTS):
            head = lax.rem(y_ref[0] + k, NY) if k < NY else NY
            source = w_ref.at[pl.ds(pl.multiple_of(head * HD, HD), HD), lanes]
            if flip == ZL and slot == NY:
                target = out_refs[-1]
            else:
                target = out_refs[flip].at[slot * HD : (slot + 1) * HD]
            copies.append(pltpu.make_async_copy(source, target, sems.at[flip, slot]))
    for copy in copies:
        copy.start()
    for copy in copies:
        copy.wait()


def project_sum(operands, terms, lanes=slice(None)):
    total = None
    for ref, low, high, weight, row in terms:
        part = jnp.dot(
            operands[ref][:, low:high],
            operands[weight][row : row + high - low, lanes],
            preferred_element_type=F32,
        )
        total = part if total is None else total + part
    return total


def project_kernel(terms, *refs):
    out_ref = refs[-1]
    total = project_sum(refs, terms)
    if len(refs) - 1 > 1 + max(term[3] for term in terms):
        total = total + refs[-2][...]
    out_ref[...] = total


def project_part(terms, *operands):
    shape = (operands[0].shape[0], operands[-1].shape[1])
    kernel = functools.partial(project_kernel, terms)
    return call(
        kernel,
        jax.ShapeDtypeStruct(shape, F32),
        *operands,
        flops=2 * shape[0] * shape[1] * sum(term[2] - term[1] for term in terms),
    )


def project_last_kernel(terms, *refs):
    operands, (out_ref, tan_ref, held_ref, sems) = refs[:-4], refs[-4:]
    rows, columns = out_ref.shape
    copies = []
    for place, start in enumerate(range(0, columns, 2 * HD)):
        lanes = slice(start, start + 2 * HD)
        total = operands[-1][:, lanes] + project_sum(operands, terms, lanes)
        held_ref[:, lanes] = total.astype(BF16)
        for half, ref in enumerate((out_ref, tan_ref)):
            source = held_ref.at[half * rows : (half + 1) * rows, lanes]
            copy = pltpu.make_async_copy(source, ref.at[:, lanes], sems.at[half, place])
            copy.start()
            copies.append(copy)
    for copy in copies:
        copy.wait()


def project_last(terms, *operands):
    rows, columns = operands[-1].shape
    return pl.pallas_call(
        functools.partial(project_last_kernel, terms),
        in_specs=[VMEM] * len(operands),
        out_specs=[HBM, HBM],
        out_shape=[jax.ShapeDtypeStruct((rows // 2, columns), BF16)] * 2,
        scratch_shapes=[
            pltpu.VMEM((rows, columns), BF16),
            pltpu.SemaphoreType.DMA((2, columns // (2 * HD))),
        ],
        name="project_last",
        compiler_params=pltpu.CompilerParams(vmem_limit_bytes=16 << 20),
    )(*operands)


def shard_step(queries, keys, values, query_tan, key_tan, value_tan, out_weight):
    rows, width = queries.shape
    heads = width // HD
    slab = keys.shape[0]
    columns = out_weight.shape[1] // (ZL * CORES)
    place = lax.axis_index("head").astype(jnp.int32).reshape(1)
    tok = lax.axis_index("tok").astype(jnp.int32).reshape(1)
    y = jnp.where(place % CORES == 0, tok % NY, tok // NY % NX)
    with_index = [SMEM] + [VMEM] * 8
    out_weight = pltpu.with_memory_space_constraint(out_weight, pltpu.HBM)
    keys, values, query_tan, key_tan, value_tan, queries = (
        pltpu.with_memory_space_constraint(array, pltpu.HBM)
        for array in (keys, values, query_tan, key_tan, value_tan, queries)
    )

    packed = call(
        pack_keys_kernel,
        jax.ShapeDtypeStruct((heads, slab, 4 * HD), BF16),
        keys,
        key_tan,
        values,
        value_tan,
        specs=[HBM] * 4,
        scratch_shapes=[pltpu.VMEM((4, slab, width), BF16), pltpu.SemaphoreType.DMA((4,))],
    )
    pieces = [packed] + [shift(packed, zh=k) for k in (1, 3, 2)]

    sends = call(
        pack_queries_kernel,
        [jax.ShapeDtypeStruct((rows, 2 * HD), BF16)] * (NY + 1),
        y,
        queries,
        query_tan,
        specs=[SMEM, HBM, HBM],
        scratch_shapes=[pltpu.VMEM((2, rows, width), BF16), pltpu.SemaphoreType.DMA((2,))],
    )
    others = [shift(sends[k], swap=k) for k in (1, 2, 3)]
    blocks = [jnp.concatenate([*others, sends[0]]), sends[NY]]

    place, _ = lax.optimization_barrier((place, sends[1]))
    cuts = call(
        cut_weight_kernel,
        [
            jax.ShapeDtypeStruct((depth, columns), BF16)
            for depth in (width, width, width - HD, width, HD)
        ],
        y,
        place,
        out_weight,
        specs=[SMEM, SMEM, HBM],
        scratch_shapes=[pltpu.SemaphoreType.DMA((ZL * CORES, NY + 1))],
    )
    pieces, cuts = lax.optimization_barrier((pieces, cuts))

    split = call(
        split_keys_kernel,
        [jax.ShapeDtypeStruct((2 * ZH * slab, 4 * HD), BF16)] * NY,
        y,
        *pieces,
        specs=with_index[: ZH + 1],
    )
    cuts, _ = lax.optimization_barrier((cuts, split[0]))
    weight_near = shift(cuts[2], zl=1)
    weight_far = across(cuts[3], core=1)
    weight_more = across(cuts[4])
    weight_core = shift(cuts[1], core=1)

    own = call(
        join_keys_kernel,
        [jax.ShapeDtypeStruct((NY * ZH * slab, 4 * HD), BF16)] * 2,
        split[0],
        *[shift(split[k], swap=k) for k in (1, 3, 2)],
    )
    left = [shift(own[0], ring=1), shift(own[1], ring=1)]
    right = [shift(own[0], ring=-1), shift(own[1], ring=-1)]
    opposite = [shift(left[0], ring=1), shift(right[1], ring=-1)]

    state = attend_step(blocks, own, ())
    state = attend_step(blocks, (left[0], right[1]), state)
    state = attend_step(blocks, (right[0], left[1]), state)
    others = call(
        attend_others_kernel,
        [jax.ShapeDtypeStruct((2 * rows, HD), BF16)] * (NY - 1),
        blocks[0],
        opposite[0],
        state[0],
        flops=3 * rows * opposite[0].shape[0] * 1792,
    )
    opposite[1], _ = lax.optimization_barrier((opposite[1], others[0]))
    kept = call(
        attend_kept_kernel,
        jax.ShapeDtypeStruct((2 * rows, 2 * HD), BF16),
        *blocks,
        *opposite,
        *state,
        flops=2 * rows * opposite[0].shape[0] * 1792,
    )

    near = [
        shift(kept, zl=1),
        jnp.concatenate([shift(others[k - 1], swap=-k, zl=1) for k in (1, 2, 3)], axis=1),
    ]
    mine = [kept, jnp.concatenate([shift(others[k - 1], swap=-k) for k in (1, 2, 3)], axis=1)]
    sibling = [shift(mine[n], core=1) for n in range(2)]
    far = [shift(near[n], core=1) for n in range(2)]
    own, rest, cut = 2 * HD, 3 * HD, width - HD
    partial = project_part(
        (
            (0, 0, own, 3, 0),
            (1, 0, own, 4, 0),
            (2, 0, cut - own, 5, own),
            (2, cut - own, rest, 6, 0),
        ),
        mine[0],
        sibling[0],
        near[1],
        cuts[0],
        weight_core,
        weight_near,
        weight_more,
    )
    partial = project_part(
        ((0, 0, rest, 3, own), (1, 0, rest, 4, own), (2, 0, own, 5, 0)),
        far[1],
        mine[1],
        near[0],
        weight_far,
        cuts[0],
        weight_near,
        partial,
    )
    return tuple(
        project_last(
            ((0, 0, rest, 2, own), (1, 0, own, 3, 0)),
            sibling[1],
            far[0],
            weight_core,
            weight_far,
            partial,
        )
    )


def solution(mesh):
    spec = P("tok", "head")
    return jax.shard_map(
        shard_step,
        mesh=mesh,
        in_specs=(spec,) * 6 + (P("head", None),),
        out_specs=(spec, spec),
        check_vma=False,
    )
```

```python
import functools

import jax
import jax.numpy as jnp
from jax import lax
from jax.experimental import pallas as pl
from jax.experimental.pallas import tpu as pltpu
from jax.sharding import PartitionSpec as P


HD = 128
SCALE = HD**-0.5
EXP2_SCALE = SCALE * 1.4426950408889634
NT = (((1,), (1,)), ((), ()))
ZH, NX, NY, ZL, CORES = 4, 4, 4, 2, 2
SLOTS = (0, NY, 1, 2, 3)
AXES = ("tok", "head")


VMEM = pl.BlockSpec(memory_space=pltpu.VMEM)
SMEM = pl.BlockSpec(memory_space=pltpu.SMEM)
HBM = pl.BlockSpec(memory_space=pltpu.HBM)
BF16 = jnp.bfloat16
F32 = jnp.float32


def shift(array, zh=0, swap=0, ring=0, zl=0, core=0):
    pairs = []
    for index in range(ZH * NX * NY * ZL * CORES):
        rest, c = divmod(index, CORES)
        rest, b = divmod(rest, ZL)
        rest, j = divmod(rest, NY)
        a, i = divmod(rest, NX)
        x, y = (swap, ring) if c else (ring, swap)
        to = ((a + zh) % ZH, (i + x) % NX, (j + y) % NY, (b + zl) % ZL, (c + core) % CORES)
        target = (((to[0] * NX + to[1]) * NY + to[2]) * ZL + to[3]) * CORES + to[4]
        pairs.append((index, target))
    return lax.ppermute(array, AXES, pairs)


def across(array):
    pairs = []
    for index in range(ZH * NX * NY * ZL * CORES):
        rest, c = divmod(index, CORES)
        rest, b = divmod(rest, ZL)
        a, xy = divmod(rest, NX * NY)
        to = (a + 1) % ZH if b else (a - 1) % ZH
        pairs.append((index, ((to * NX * NY + xy) * ZL + 1 - b) * CORES + 1 - c))
    return lax.ppermute(array, AXES, pairs)


def call(kernel, outs, *operands, flops=0, specs=None, limit=16, **kwargs):
    return called(kernel, outs, operands, flops, specs, limit, kwargs)


def called(kernel, outs, operands, flops, specs, limit, kwargs):
    return pl.pallas_call(
        kernel,
        out_shape=outs,
        in_specs=specs or [VMEM] * len(operands),
        out_specs=jax.tree.map(lambda _: VMEM, outs),
        compiler_params=pltpu.CompilerParams(vmem_limit_bytes=limit << 20),
        cost_estimate=pl.CostEstimate(
            flops=flops,
            transcendentals=0,
            bytes_accessed=sum(o.size * o.dtype.itemsize for o in operands),
        ),
        **kwargs,
    )(*operands)


def fetch(source_refs, held_ref, sems):
    copies = [
        pltpu.make_async_copy(ref, held_ref.at[slot], sems.at[slot]) for slot, ref in enumerate(source_refs)
    ]
    for copy in copies:
        copy.start()
    for copy in copies:
        copy.wait()


def pack_keys_kernel(k_ref, dk_ref, v_ref, dv_ref, out_ref, held_ref, sems):
    fetch((k_ref, dk_ref, v_ref, dv_ref), held_ref, sems)
    for head in range(out_ref.shape[0]):
        for slot in range(4):
            out_ref[head, :, slot * HD : (slot + 1) * HD] = held_ref[slot, :, head * HD : (head + 1) * HD]


def pack_queries_kernel(y_ref, q_ref, dq_ref, *refs):
    out_refs, (held_ref, sems) = refs[:-2], refs[-2:]
    fetch((dq_ref, q_ref), held_ref, sems)
    for k, out_ref in enumerate(out_refs):
        head = lax.rem(y_ref[0] + k, NY) if k < NY else NY
        lanes = pl.ds(pl.multiple_of(head * HD, HD), HD)
        out_ref[:, :HD] = held_ref[0, :, lanes]
        out_ref[:, HD:] = held_ref[1, :, lanes]


def split_keys_kernel(y_ref, *refs):
    pieces, out_refs = refs[:ZH], refs[ZH:]
    for k, out_ref in enumerate(out_refs):
        for half, head in enumerate((lax.rem(y_ref[0] + k, NY), NY)):
            for z, piece in enumerate(pieces):
                rows = piece.shape[1]
                start = (half * ZH + z) * rows
                out_ref[start : start + rows, :] = piece[head]


def join_keys_kernel(*refs):
    pieces, out_refs = refs[:NY], refs[NY:]
    rows = pieces[0].shape[0] // 2
    for half, out_ref in enumerate(out_refs):
        for k, piece in enumerate(pieces):
            out_ref[k * rows : (k + 1) * rows, :] = piece[half * rows : (half + 1) * rows, :]


def attend(both, key_ref, state):
    query = both[:, HD:]
    keys = key_ref[:, : 2 * HD]
    values = key_ref[:, 2 * HD :]
    scores = lax.dot_general(query, keys[:, :HD], NT, preferred_element_type=F32)
    tangent = lax.dot_general(both, keys, NT, preferred_element_type=F32)
    top = jnp.max(scores, axis=1, keepdims=True)
    if state is None:
        peak = jnp.broadcast_to(top, (scores.shape[0], HD))
    else:
        peak_old, total, total_tan, numer, numer_tan = state
        peak = jnp.maximum(peak_old, top)
        fade = jnp.exp2((peak_old - peak) * EXP2_SCALE)
    expo = jnp.exp2((scores - peak[:, :1]) * EXP2_SCALE)
    expo_tan = expo * tangent
    cuts = range(0, scores.shape[1], HD)
    add = sum(expo[:, c : c + HD] for c in cuts)
    add_tan = sum(expo_tan[:, c : c + HD] for c in cuts)
    pair = jnp.dot(expo.astype(BF16), values, preferred_element_type=F32)
    single = jnp.dot(expo_tan.astype(BF16), values[:, :HD], preferred_element_type=F32)
    if state is None:
        return peak, add, add_tan, pair, single
    return (
        peak,
        total * fade + add,
        total_tan * fade + add_tan,
        numer * jnp.concatenate([fade, fade], axis=1) + pair,
        numer_tan * fade + single,
    )


def finish(state):
    _, total, total_tan, numer, numer_tan = state
    inverse = 1.0 / jnp.sum(total, axis=1, keepdims=True)
    total_tan = jnp.sum(total_tan, axis=1, keepdims=True) * SCALE
    attended = numer[:, :HD] * inverse
    attended_tan = (numer_tan * SCALE + numer[:, HD:] - attended * total_tan) * inverse
    return attended.astype(BF16), attended_tan.astype(BF16)


def load_state(ref, rows):
    cut = [ref[rows, c * HD : (c + 1) * HD] for c in range(3)]
    return (*cut, ref[rows, 3 * HD : 5 * HD], ref[rows, 5 * HD :])


def attend_begin_kernel(shared_ref, own_ref, shared_keys, own_keys, *out_refs):
    sides = ((shared_ref, shared_keys), (own_ref, own_keys))
    for (query, keys), out_ref in zip(sides, out_refs):
        out_ref[...] = jnp.concatenate(attend(query[...], keys, None), axis=1)


def attend_more_kernel(query_ref, keys, state_ref, out_ref):
    state = load_state(state_ref, slice(None))
    out_ref[...] = jnp.concatenate(attend(query_ref[...], keys, state), axis=1)


def attend_more(query, keys, state):
    return call(
        attend_more_kernel,
        jax.ShapeDtypeStruct(state.shape, F32),
        query,
        keys,
        state,
        flops=query.shape[0] * keys.shape[0] * 1792,
    )


def attend_done_kernel(start, query_ref, keys, state_ref, *out_refs):
    rows = out_refs[0].shape[0] // 2
    part = slice(start, start + rows * len(out_refs))
    attended, attended_tan = finish(attend(query_ref[part, :], keys, load_state(state_ref, part)))
    for place, ref in enumerate(out_refs):
        ref[:rows, :] = attended[place * rows : (place + 1) * rows]
        ref[rows:, :] = attended_tan[place * rows : (place + 1) * rows]


def attend_done(query, keys, state, start, rows, count):
    return call(
        functools.partial(attend_done_kernel, start),
        [jax.ShapeDtypeStruct((2 * rows, HD), BF16)] * count,
        query,
        keys,
        state,
        flops=count * rows * keys.shape[0] * 1792,
    )


def attend_last_kernel(query_ref, b_keys, c_keys, d_keys, state_ref, done_ref, out_ref):
    rows = query_ref.shape[0]
    state = load_state(state_ref, slice(None))
    for keys in (b_keys, c_keys, d_keys):
        state = attend(query_ref[...], keys, state)
    out_ref[:, :HD] = done_ref[...]
    out_ref[:rows, HD:], out_ref[rows:, HD:] = finish(state)


def cut_weight_kernel(y_ref, place_ref, w_ref, *refs):
    out_refs, sems = refs[:-1], refs[-1]
    columns = out_refs[0].shape[1]
    copies = []
    for flip in range(ZL * CORES):
        block = lax.bitwise_xor(place_ref[0], flip)
        lanes = pl.ds(pl.multiple_of(block * columns, HD), columns)
        for slot, k in enumerate(SLOTS):
            head = lax.rem(y_ref[0] + k, NY) if k < NY else NY
            source = w_ref.at[pl.ds(pl.multiple_of(head * HD, HD), HD), lanes]
            target = out_refs[flip].at[slot * HD : (slot + 1) * HD]
            copies.append(pltpu.make_async_copy(source, target, sems.at[flip, slot]))
    for copy in copies:
        copy.start()
    for copy in copies:
        copy.wait()


def project_sum(operands, terms, lanes=slice(None)):
    total = None
    for ref, low, high, weight, row in terms:
        part = jnp.dot(
            operands[ref][:, low:high],
            operands[weight][row : row + high - low, lanes],
            preferred_element_type=F32,
        )
        total = part if total is None else total + part
    return total


def project_kernel(terms, *refs):
    out_ref = refs[-1]
    total = project_sum(refs, terms)
    if len(refs) - 1 > 1 + max(term[3] for term in terms):
        total = total + refs[-2][...]
    out_ref[...] = total


def project_part(terms, *operands):
    shape = (operands[0].shape[0], operands[-1].shape[1])
    kernel = functools.partial(project_kernel, terms)
    return call(
        kernel,
        jax.ShapeDtypeStruct(shape, F32),
        *operands,
        flops=2 * shape[0] * shape[1] * sum(term[2] - term[1] for term in terms),
    )


def project_last_kernel(terms, *refs):
    operands, (out_ref, tan_ref, held_ref, sems) = refs[:-4], refs[-4:]
    rows, columns = out_ref.shape
    copies = []
    for place, start in enumerate(range(0, columns, 2 * HD)):
        lanes = slice(start, start + 2 * HD)
        total = operands[-1][:, lanes] + project_sum(operands, terms, lanes)
        held_ref[:, lanes] = total.astype(BF16)
        for half, ref in enumerate((out_ref, tan_ref)):
            source = held_ref.at[half * rows : (half + 1) * rows, lanes]
            copy = pltpu.make_async_copy(source, ref.at[:, lanes], sems.at[half, place])
            copy.start()
            copies.append(copy)
    for copy in copies:
        copy.wait()


def project_last(terms, *operands):
    rows, columns = operands[-1].shape
    return pl.pallas_call(
        functools.partial(project_last_kernel, terms),
        in_specs=[VMEM] * len(operands),
        out_specs=[HBM, HBM],
        out_shape=[jax.ShapeDtypeStruct((rows // 2, columns), BF16)] * 2,
        scratch_shapes=[
            pltpu.VMEM((rows, columns), BF16),
            pltpu.SemaphoreType.DMA((2, columns // (2 * HD))),
        ],
        name="project_last",
        compiler_params=pltpu.CompilerParams(vmem_limit_bytes=16 << 20),
    )(*operands)


def shard_step(queries, keys, values, query_tan, key_tan, value_tan, out_weight):
    rows, width = queries.shape
    heads = width // HD
    slab = keys.shape[0]
    columns = out_weight.shape[1] // (ZL * CORES)
    place = lax.axis_index("head").astype(jnp.int32).reshape(1)
    tok = lax.axis_index("tok").astype(jnp.int32).reshape(1)
    y = jnp.where(place % CORES == 0, tok % NY, tok // NY % NX)
    with_index = [SMEM] + [VMEM] * 8
    out_weight = pltpu.with_memory_space_constraint(out_weight, pltpu.HBM)
    keys, values, query_tan, key_tan, value_tan, queries = (
        pltpu.with_memory_space_constraint(array, pltpu.HBM)
        for array in (keys, values, query_tan, key_tan, value_tan, queries)
    )

    packed = call(
        pack_keys_kernel,
        jax.ShapeDtypeStruct((heads, slab, 4 * HD), BF16),
        keys,
        key_tan,
        values,
        value_tan,
        specs=[HBM] * 4,
        scratch_shapes=[pltpu.VMEM((4, slab, width), BF16), pltpu.SemaphoreType.DMA((4,))],
    )
    pieces = [packed] + [shift(packed, zh=k) for k in (1, 3, 2)]

    sends = call(
        pack_queries_kernel,
        [jax.ShapeDtypeStruct((rows, 2 * HD), BF16)] * (NY + 1),
        y,
        queries,
        query_tan,
        specs=[SMEM, HBM, HBM],
        scratch_shapes=[pltpu.VMEM((2, rows, width), BF16), pltpu.SemaphoreType.DMA((2,))],
    )
    others = [shift(sends[k], swap=k) for k in (1, 2, 3)]
    blocks = [jnp.concatenate([*others, sends[0]]), sends[NY]]

    place, _ = lax.optimization_barrier((place, sends[1]))
    cuts = call(
        cut_weight_kernel,
        [jax.ShapeDtypeStruct((width, columns), BF16)] * (ZL * CORES),
        y,
        place,
        out_weight,
        specs=[SMEM, SMEM, HBM],
        scratch_shapes=[pltpu.SemaphoreType.DMA((ZL * CORES, NY + 1))],
    )
    pieces, cuts = lax.optimization_barrier((pieces, cuts))

    split = call(
        split_keys_kernel,
        [jax.ShapeDtypeStruct((2 * ZH * slab, 4 * HD), BF16)] * NY,
        y,
        *pieces,
        specs=with_index[: ZH + 1],
    )
    cuts, _ = lax.optimization_barrier((cuts, split[0]))
    weight_near = shift(cuts[2], zl=1)
    weight_far = across(cuts[3])
    weight_core = shift(cuts[1], core=1)

    own = call(
        join_keys_kernel,
        [jax.ShapeDtypeStruct((NY * ZH * slab, 4 * HD), BF16)] * 2,
        split[0],
        *[shift(split[k], swap=k) for k in (1, 3, 2)],
    )
    left = [shift(own[0], ring=1), shift(own[1], ring=1)]
    right = [shift(own[0], ring=-1), shift(own[1], ring=-1)]
    opposite = [shift(left[0], ring=1), shift(right[1], ring=-1)]

    state, own_state = call(
        attend_begin_kernel,
        [jax.ShapeDtypeStruct((block.shape[0], 6 * HD), F32) for block in blocks],
        *blocks,
        *own,
        flops=(NY + 1) * rows * own[0].shape[0] * 1792,
    )
    state = attend_more(blocks[0], left[0], state)
    state = attend_more(blocks[0], right[0], state)
    peers = NY - 1
    others = attend_done(blocks[0], opposite[0], state, 0, rows, peers)
    last_keys, _ = lax.optimization_barrier((opposite[0], others[0]))
    kept = attend_done(blocks[0], last_keys, state, peers * rows, rows, 1)
    kept = call(
        attend_last_kernel,
        jax.ShapeDtypeStruct((2 * rows, 2 * HD), BF16),
        blocks[1],
        right[1],
        left[1],
        opposite[1],
        own_state,
        *kept,
        flops=3 * rows * opposite[1].shape[0] * 1792,
    )

    near = [
        shift(kept, zl=1),
        jnp.concatenate([shift(others[k - 1], swap=-k, zl=1) for k in (1, 2, 3)], axis=1),
    ]
    mine = [kept, jnp.concatenate([shift(others[k - 1], swap=-k) for k in (1, 2, 3)], axis=1)]
    sibling = [shift(mine[n], core=1) for n in range(2)]
    far = [shift(near[n], core=1) for n in range(2)]
    own, rest = 2 * HD, 3 * HD
    partial = project_part(
        (
            (0, 0, own, 3, 0),
            (1, 0, own, 4, 0),
            (2, 0, rest, 5, own),
        ),
        mine[0],
        sibling[0],
        near[1],
        cuts[0],
        weight_core,
        weight_near,
    )
    partial = project_part(
        ((0, 0, rest, 3, own), (1, 0, rest, 4, own), (2, 0, own, 5, 0)),
        far[1],
        mine[1],
        near[0],
        weight_far,
        cuts[0],
        weight_near,
        partial,
    )
    return tuple(
        project_last(
            ((0, 0, rest, 2, own), (1, 0, own, 3, 0)),
            sibling[1],
            far[0],
            weight_core,
            weight_far,
            partial,
        )
    )


def solution(mesh):
    spec = P("tok", "head")
    return jax.shard_map(
        shard_step,
        mesh=mesh,
        in_specs=(spec,) * 6 + (P("head", None),),
        out_specs=(spec, spec),
        check_vma=False,
    )
```

```python
import functools

import jax
import jax.numpy as jnp
from jax import lax
from jax.experimental import pallas as pl
from jax.experimental.pallas import tpu as pltpu
from jax.sharding import PartitionSpec as P


HD = 128
SCALE = HD**-0.5
EXP2_SCALE = SCALE * 1.4426950408889634
NT = (((1,), (1,)), ((), ()))
ZH, NX, NY, ZL, CORES = 4, 4, 4, 2, 2
SLOTS = (0, NY, 1, 2, 3)
AXES = ("tok", "head")


VMEM = pl.BlockSpec(memory_space=pltpu.VMEM)
SMEM = pl.BlockSpec(memory_space=pltpu.SMEM)
HBM = pl.BlockSpec(memory_space=pltpu.HBM)
BF16 = jnp.bfloat16
F32 = jnp.float32


def shift(array, zh=0, swap=0, ring=0, zl=0, core=0):
    pairs = []
    for index in range(ZH * NX * NY * ZL * CORES):
        rest, c = divmod(index, CORES)
        rest, b = divmod(rest, ZL)
        rest, j = divmod(rest, NY)
        a, i = divmod(rest, NX)
        x, y = (swap, ring) if c else (ring, swap)
        to = ((a + zh) % ZH, (i + x) % NX, (j + y) % NY, (b + zl) % ZL, (c + core) % CORES)
        target = (((to[0] * NX + to[1]) * NY + to[2]) * ZL + to[3]) * CORES + to[4]
        pairs.append((index, target))
    return lax.ppermute(array, AXES, pairs)


def across(array):
    pairs = []
    for index in range(ZH * NX * NY * ZL * CORES):
        rest, c = divmod(index, CORES)
        rest, b = divmod(rest, ZL)
        a, xy = divmod(rest, NX * NY)
        to = (a + 1) % ZH if b else (a - 1) % ZH
        pairs.append((index, ((to * NX * NY + xy) * ZL + 1 - b) * CORES + 1 - c))
    return lax.ppermute(array, AXES, pairs)


def call(kernel, outs, *operands, flops=0, specs=None, limit=16, **kwargs):
    return called(kernel, outs, operands, flops, specs, limit, kwargs)


def called(kernel, outs, operands, flops, specs, limit, kwargs):
    return pl.pallas_call(
        kernel,
        out_shape=outs,
        in_specs=specs or [VMEM] * len(operands),
        out_specs=jax.tree.map(lambda _: VMEM, outs),
        compiler_params=pltpu.CompilerParams(vmem_limit_bytes=limit << 20),
        cost_estimate=pl.CostEstimate(
            flops=flops,
            transcendentals=0,
            bytes_accessed=sum(o.size * o.dtype.itemsize for o in operands),
        ),
        **kwargs,
    )(*operands)


def fetch(source_refs, held_ref, sems):
    copies = [
        pltpu.make_async_copy(ref, held_ref.at[slot], sems.at[slot]) for slot, ref in enumerate(source_refs)
    ]
    for copy in copies:
        copy.start()
    for copy in copies:
        copy.wait()


def pack_keys_kernel(k_ref, dk_ref, v_ref, dv_ref, out_ref, held_ref, sems):
    fetch((k_ref, dk_ref, v_ref, dv_ref), held_ref, sems)
    for head in range(out_ref.shape[0]):
        for slot in range(4):
            out_ref[head, :, slot * HD : (slot + 1) * HD] = held_ref[slot, :, head * HD : (head + 1) * HD]


def pack_queries_kernel(y_ref, q_ref, dq_ref, *refs):
    out_refs, (held_ref, sems) = refs[:-2], refs[-2:]
    fetch((dq_ref, q_ref), held_ref, sems)
    for k, out_ref in enumerate(out_refs):
        head = lax.rem(y_ref[0] + k, NY) if k < NY else NY
        lanes = pl.ds(pl.multiple_of(head * HD, HD), HD)
        out_ref[:, :HD] = held_ref[0, :, lanes]
        out_ref[:, HD:] = held_ref[1, :, lanes]


def split_keys_kernel(y_ref, *refs):
    pieces, out_refs = refs[:ZH], refs[ZH:]
    for k, out_ref in enumerate(out_refs):
        for half, head in enumerate((lax.rem(y_ref[0] + k, NY), NY)):
            for z, piece in enumerate(pieces):
                rows = piece.shape[1]
                start = (half * ZH + z) * rows
                out_ref[start : start + rows, :] = piece[head]


def join_keys_kernel(*refs):
    pieces, out_refs = refs[:NY], refs[NY:]
    rows = pieces[0].shape[0] // 2
    for half, out_ref in enumerate(out_refs):
        for k, piece in enumerate(pieces):
            out_ref[k * rows : (k + 1) * rows, :] = piece[half * rows : (half + 1) * rows, :]


def attend(both, key_ref, state):
    query = both[:, HD:]
    keys = key_ref[:, : 2 * HD]
    values = key_ref[:, 2 * HD :]
    scores = lax.dot_general(query, keys[:, :HD], NT, preferred_element_type=F32)
    tangent = lax.dot_general(both, keys, NT, preferred_element_type=F32)
    top = jnp.max(scores, axis=1, keepdims=True)
    if state is None:
        peak = jnp.broadcast_to(top, (scores.shape[0], HD))
    else:
        peak_old, total, total_tan, numer, numer_tan = state
        peak = jnp.maximum(peak_old, top)
        fade = jnp.exp2((peak_old - peak) * EXP2_SCALE)
    expo = jnp.exp2((scores - peak[:, :1]) * EXP2_SCALE)
    expo_tan = expo * tangent
    cuts = range(0, scores.shape[1], HD)
    add = sum(expo[:, c : c + HD] for c in cuts)
    add_tan = sum(expo_tan[:, c : c + HD] for c in cuts)
    pair = jnp.dot(expo.astype(BF16), values, preferred_element_type=F32)
    single = jnp.dot(expo_tan.astype(BF16), values[:, :HD], preferred_element_type=F32)
    if state is None:
        return peak, add, add_tan, pair, single
    return (
        peak,
        total * fade + add,
        total_tan * fade + add_tan,
        numer * jnp.concatenate([fade, fade], axis=1) + pair,
        numer_tan * fade + single,
    )


def finish(state):
    _, total, total_tan, numer, numer_tan = state
    inverse = 1.0 / jnp.sum(total, axis=1, keepdims=True)
    total_tan = jnp.sum(total_tan, axis=1, keepdims=True) * SCALE
    attended = numer[:, :HD] * inverse
    attended_tan = (numer_tan * SCALE + numer[:, HD:] - attended * total_tan) * inverse
    return attended.astype(BF16), attended_tan.astype(BF16)


def load_state(ref, rows):
    cut = [ref[rows, c * HD : (c + 1) * HD] for c in range(3)]
    return (*cut, ref[rows, 3 * HD : 5 * HD], ref[rows, 5 * HD :])


def attend_kernel(first, shared_ref, own_ref, shared_keys, own_keys, *refs):
    sides = ((shared_ref, shared_keys, refs[-2]), (own_ref, own_keys, refs[-1]))
    for side, (query, keys, out_ref) in enumerate(sides):
        state = None if first else load_state(refs[side], slice(None))
        out_ref[...] = jnp.concatenate(attend(query[...], keys, state), axis=1)


def attend_step(queries, keys, state):
    rows = [query.shape[0] for query in queries]
    return call(
        functools.partial(attend_kernel, not state),
        [jax.ShapeDtypeStruct((n, 6 * HD), F32) for n in rows],
        *queries,
        *keys,
        *state,
        flops=sum(rows) * keys[0].shape[0] * 1792,
    )


def attend_done_kernel(start, query_ref, keys, state_ref, *out_refs):
    rows = out_refs[0].shape[0] // 2
    part = slice(start, start + rows * len(out_refs))
    attended, attended_tan = finish(attend(query_ref[part, :], keys, load_state(state_ref, part)))
    for place, ref in enumerate(out_refs):
        ref[:rows, :] = attended[place * rows : (place + 1) * rows]
        ref[rows:, :] = attended_tan[place * rows : (place + 1) * rows]


def attend_done(query, keys, state, start, rows, count):
    return call(
        functools.partial(attend_done_kernel, start),
        [jax.ShapeDtypeStruct((2 * rows, HD), BF16)] * count,
        query,
        keys,
        state,
        flops=count * rows * keys.shape[0] * 1792,
    )


def attend_kept_kernel(shared_ref, own_ref, shared_keys, own_keys, shared_state, own_state, out_ref):
    rows = own_ref.shape[0]
    start = shared_ref.shape[0] - rows
    sides = (
        (shared_ref, shared_keys, shared_state, slice(start, start + rows)),
        (own_ref, own_keys, own_state, slice(0, rows)),
    )
    for side, (query, keys, state, part) in enumerate(sides):
        lanes = slice(side * HD, (side + 1) * HD)
        attended, attended_tan = finish(attend(query[part, :], keys, load_state(state, part)))
        out_ref[:rows, lanes] = attended
        out_ref[rows:, lanes] = attended_tan


def cut_weight_kernel(y_ref, place_ref, w_ref, *refs):
    out_refs, sems = refs[:-1], refs[-1]
    columns = out_refs[0].shape[1]
    copies = []
    for flip in range(ZL * CORES):
        block = lax.bitwise_xor(place_ref[0], flip)
        lanes = pl.ds(pl.multiple_of(block * columns, HD), columns)
        for slot, k in enumerate(SLOTS):
            head = lax.rem(y_ref[0] + k, NY) if k < NY else NY
            source = w_ref.at[pl.ds(pl.multiple_of(head * HD, HD), HD), lanes]
            target = out_refs[flip].at[slot * HD : (slot + 1) * HD]
            copies.append(pltpu.make_async_copy(source, target, sems.at[flip, slot]))
    for copy in copies:
        copy.start()
    for copy in copies:
        copy.wait()


def project_sum(operands, terms, lanes=slice(None)):
    total = None
    for ref, low, high, weight, row in terms:
        part = jnp.dot(
            operands[ref][:, low:high],
            operands[weight][row : row + high - low, lanes],
            preferred_element_type=F32,
        )
        total = part if total is None else total + part
    return total


def project_kernel(terms, *refs):
    out_ref = refs[-1]
    total = project_sum(refs, terms)
    if len(refs) - 1 > 1 + max(term[3] for term in terms):
        total = total + refs[-2][...]
    out_ref[...] = total


def project_part(terms, *operands):
    shape = (operands[0].shape[0], operands[-1].shape[1])
    kernel = functools.partial(project_kernel, terms)
    return call(
        kernel,
        jax.ShapeDtypeStruct(shape, F32),
        *operands,
        flops=2 * shape[0] * shape[1] * sum(term[2] - term[1] for term in terms),
    )


def project_last_kernel(terms, *refs):
    operands, (out_ref, tan_ref, held_ref, sems) = refs[:-4], refs[-4:]
    rows, columns = out_ref.shape
    copies = []
    for place, start in enumerate(range(0, columns, 2 * HD)):
        lanes = slice(start, start + 2 * HD)
        total = operands[-1][:, lanes] + project_sum(operands, terms, lanes)
        held_ref[:, lanes] = total.astype(BF16)
        for half, ref in enumerate((out_ref, tan_ref)):
            source = held_ref.at[half * rows : (half + 1) * rows, lanes]
            copy = pltpu.make_async_copy(source, ref.at[:, lanes], sems.at[half, place])
            copy.start()
            copies.append(copy)
    for copy in copies:
        copy.wait()


def project_last(terms, *operands):
    rows, columns = operands[-1].shape
    return pl.pallas_call(
        functools.partial(project_last_kernel, terms),
        in_specs=[VMEM] * len(operands),
        out_specs=[HBM, HBM],
        out_shape=[jax.ShapeDtypeStruct((rows // 2, columns), BF16)] * 2,
        scratch_shapes=[
            pltpu.VMEM((rows, columns), BF16),
            pltpu.SemaphoreType.DMA((2, columns // (2 * HD))),
        ],
        name="project_last",
        compiler_params=pltpu.CompilerParams(vmem_limit_bytes=16 << 20),
    )(*operands)


def shard_step(queries, keys, values, query_tan, key_tan, value_tan, out_weight):
    rows, width = queries.shape
    heads = width // HD
    slab = keys.shape[0]
    columns = out_weight.shape[1] // (ZL * CORES)
    place = lax.axis_index("head").astype(jnp.int32).reshape(1)
    tok = lax.axis_index("tok").astype(jnp.int32).reshape(1)
    y = jnp.where(place % CORES == 0, tok % NY, tok // NY % NX)
    with_index = [SMEM] + [VMEM] * 8
    out_weight = pltpu.with_memory_space_constraint(out_weight, pltpu.HBM)
    keys, values, query_tan, key_tan, value_tan, queries = (
        pltpu.with_memory_space_constraint(array, pltpu.HBM)
        for array in (keys, values, query_tan, key_tan, value_tan, queries)
    )

    packed = call(
        pack_keys_kernel,
        jax.ShapeDtypeStruct((heads, slab, 4 * HD), BF16),
        keys,
        key_tan,
        values,
        value_tan,
        specs=[HBM] * 4,
        scratch_shapes=[pltpu.VMEM((4, slab, width), BF16), pltpu.SemaphoreType.DMA((4,))],
    )
    pieces = [packed] + [shift(packed, zh=k) for k in (1, 3, 2)]

    sends = call(
        pack_queries_kernel,
        [jax.ShapeDtypeStruct((rows, 2 * HD), BF16)] * (NY + 1),
        y,
        queries,
        query_tan,
        specs=[SMEM, HBM, HBM],
        scratch_shapes=[pltpu.VMEM((2, rows, width), BF16), pltpu.SemaphoreType.DMA((2,))],
    )
    others = [shift(sends[k], swap=k) for k in (1, 2, 3)]
    blocks = [jnp.concatenate([*others, sends[0]]), sends[NY]]

    place, _ = lax.optimization_barrier((place, sends[1]))
    cuts = call(
        cut_weight_kernel,
        [jax.ShapeDtypeStruct((width, columns), BF16)] * (ZL * CORES),
        y,
        place,
        out_weight,
        specs=[SMEM, SMEM, HBM],
        scratch_shapes=[pltpu.SemaphoreType.DMA((ZL * CORES, NY + 1))],
    )
    pieces, cuts = lax.optimization_barrier((pieces, cuts))

    split = call(
        split_keys_kernel,
        [jax.ShapeDtypeStruct((2 * ZH * slab, 4 * HD), BF16)] * NY,
        y,
        *pieces,
        specs=with_index[: ZH + 1],
    )
    cuts, _ = lax.optimization_barrier((cuts, split[0]))
    weight_near = shift(cuts[2], zl=1)
    weight_far = across(cuts[3])
    weight_core = shift(cuts[1], core=1)

    own = call(
        join_keys_kernel,
        [jax.ShapeDtypeStruct((NY * ZH * slab, 4 * HD), BF16)] * 2,
        split[0],
        *[shift(split[k], swap=k) for k in (1, 3, 2)],
    )
    left = [shift(own[0], ring=1), shift(own[1], ring=1)]
    right = [shift(own[0], ring=-1), shift(own[1], ring=-1)]
    opposite = [shift(left[0], ring=1), shift(right[1], ring=-1)]

    state = attend_step(blocks, own, ())
    state = attend_step(blocks, (left[0], right[1]), state)
    state = attend_step(blocks, (right[0], left[1]), state)
    others = attend_done(blocks[0], opposite[0], state[0], 0, rows, 1)
    opposite[0], _ = lax.optimization_barrier((opposite[0], others[0]))
    others += attend_done(blocks[0], opposite[0], state[0], rows, rows, NY - 2)
    opposite[1], _ = lax.optimization_barrier((opposite[1], others[-1]))
    kept = call(
        attend_kept_kernel,
        jax.ShapeDtypeStruct((2 * rows, 2 * HD), BF16),
        *blocks,
        *opposite,
        *state,
        flops=2 * rows * opposite[0].shape[0] * 1792,
    )

    near = [
        shift(kept, zl=1),
        jnp.concatenate([shift(others[k - 1], swap=-k, zl=1) for k in (1, 2, 3)], axis=1),
    ]
    mine = [kept, jnp.concatenate([shift(others[k - 1], swap=-k) for k in (1, 2, 3)], axis=1)]
    sibling = [shift(mine[n], core=1) for n in range(2)]
    far = [shift(near[n], core=1) for n in range(2)]
    own, rest = 2 * HD, 3 * HD
    partial = project_part(
        (
            (0, 0, own, 3, 0),
            (1, 0, own, 4, 0),
            (2, 0, rest, 5, own),
        ),
        mine[0],
        sibling[0],
        near[1],
        cuts[0],
        weight_core,
        weight_near,
    )
    partial = project_part(
        ((0, 0, rest, 3, own), (1, 0, rest, 4, own), (2, 0, own, 5, 0)),
        far[1],
        mine[1],
        near[0],
        weight_far,
        cuts[0],
        weight_near,
        partial,
    )
    return tuple(
        project_last(
            ((0, 0, rest, 2, own), (1, 0, own, 3, 0)),
            sibling[1],
            far[0],
            weight_core,
            weight_far,
            partial,
        )
    )


def solution(mesh):
    spec = P("tok", "head")
    return jax.shard_map(
        shard_step,
        mesh=mesh,
        in_specs=(spec,) * 6 + (P("head", None),),
        out_specs=(spec, spec),
        check_vma=False,
    )
```

```python
import functools

import jax
import jax.numpy as jnp
from jax import lax
from jax.experimental import pallas as pl
from jax.experimental.pallas import tpu as pltpu
from jax.sharding import PartitionSpec as P


HD = 128
SCALE = HD**-0.5
EXP2_SCALE = SCALE * 1.4426950408889634
NT = (((1,), (1,)), ((), ()))
ZH, NX, NY, ZL, CORES = 4, 4, 4, 2, 2
SLOTS = (0, NY, 1, 2, 3)
AXES = ("tok", "head")


VMEM = pl.BlockSpec(memory_space=pltpu.VMEM)
SMEM = pl.BlockSpec(memory_space=pltpu.SMEM)
HBM = pl.BlockSpec(memory_space=pltpu.HBM)
BF16 = jnp.bfloat16
F32 = jnp.float32


def shift(array, zh=0, swap=0, ring=0, zl=0, core=0):
    pairs = []
    for index in range(ZH * NX * NY * ZL * CORES):
        rest, c = divmod(index, CORES)
        rest, b = divmod(rest, ZL)
        rest, j = divmod(rest, NY)
        a, i = divmod(rest, NX)
        x, y = (swap, ring) if c else (ring, swap)
        to = ((a + zh) % ZH, (i + x) % NX, (j + y) % NY, (b + zl) % ZL, (c + core) % CORES)
        target = (((to[0] * NX + to[1]) * NY + to[2]) * ZL + to[3]) * CORES + to[4]
        pairs.append((index, target))
    return lax.ppermute(array, AXES, pairs)


def across(array):
    pairs = []
    for index in range(ZH * NX * NY * ZL * CORES):
        rest, c = divmod(index, CORES)
        rest, b = divmod(rest, ZL)
        a, xy = divmod(rest, NX * NY)
        to = (a + 1) % ZH if b else (a - 1) % ZH
        pairs.append((index, ((to * NX * NY + xy) * ZL + 1 - b) * CORES + 1 - c))
    return lax.ppermute(array, AXES, pairs)


def call(kernel, outs, *operands, flops=0, specs=None, limit=16, **kwargs):
    return called(kernel, outs, operands, flops, specs, limit, kwargs)


def called(kernel, outs, operands, flops, specs, limit, kwargs):
    return pl.pallas_call(
        kernel,
        out_shape=outs,
        in_specs=specs or [VMEM] * len(operands),
        out_specs=jax.tree.map(lambda _: VMEM, outs),
        compiler_params=pltpu.CompilerParams(vmem_limit_bytes=limit << 20),
        cost_estimate=pl.CostEstimate(
            flops=flops,
            transcendentals=0,
            bytes_accessed=sum(o.size * o.dtype.itemsize for o in operands),
        ),
        **kwargs,
    )(*operands)


def fetch(source_refs, held_ref, sems):
    copies = [
        pltpu.make_async_copy(ref, held_ref.at[slot], sems.at[slot]) for slot, ref in enumerate(source_refs)
    ]
    for copy in copies:
        copy.start()
    for copy in copies:
        copy.wait()


def pack_keys_kernel(k_ref, dk_ref, v_ref, dv_ref, out_ref, held_ref, sems):
    fetch((k_ref, dk_ref, v_ref, dv_ref), held_ref, sems)
    for head in range(out_ref.shape[0]):
        for slot in range(4):
            out_ref[head, :, slot * HD : (slot + 1) * HD] = held_ref[slot, :, head * HD : (head + 1) * HD]


def pack_queries_kernel(y_ref, q_ref, dq_ref, *refs):
    out_refs, (held_ref, sems) = refs[:-2], refs[-2:]
    fetch((dq_ref, q_ref), held_ref, sems)
    for k, out_ref in enumerate(out_refs):
        head = lax.rem(y_ref[0] + k, NY) if k < NY else NY
        lanes = pl.ds(pl.multiple_of(head * HD, HD), HD)
        out_ref[:, :HD] = held_ref[0, :, lanes]
        out_ref[:, HD:] = held_ref[1, :, lanes]


def split_keys_kernel(y_ref, *refs):
    pieces, out_refs = refs[:ZH], refs[ZH:]
    for k, out_ref in enumerate(out_refs):
        for half, head in enumerate((lax.rem(y_ref[0] + k, NY), NY)):
            for z, piece in enumerate(pieces):
                rows = piece.shape[1]
                start = (half * ZH + z) * rows
                out_ref[start : start + rows, :] = piece[head]


def join_keys_kernel(*refs):
    pieces, out_refs = refs[:NY], refs[NY:]
    rows = pieces[0].shape[0] // 2
    for half, out_ref in enumerate(out_refs):
        for k, piece in enumerate(pieces):
            out_ref[k * rows : (k + 1) * rows, :] = piece[half * rows : (half + 1) * rows, :]


def attend(both, key_ref, state):
    query = both[:, HD:]
    keys = key_ref[:, : 2 * HD]
    values = key_ref[:, 2 * HD :]
    scores = lax.dot_general(query, keys[:, :HD], NT, preferred_element_type=F32)
    tangent = lax.dot_general(both, keys, NT, preferred_element_type=F32)
    top = jnp.max(scores, axis=1, keepdims=True)
    if state is None:
        peak = jnp.broadcast_to(top, (scores.shape[0], HD))
    else:
        peak_old, total, total_tan, numer, numer_tan = state
        peak = jnp.maximum(peak_old, top)
        fade = jnp.exp2((peak_old - peak) * EXP2_SCALE)
    expo = jnp.exp2((scores - peak[:, :1]) * EXP2_SCALE)
    expo_tan = expo * tangent
    cuts = range(0, scores.shape[1], HD)
    add = sum(expo[:, c : c + HD] for c in cuts)
    add_tan = sum(expo_tan[:, c : c + HD] for c in cuts)
    pair = jnp.dot(expo.astype(BF16), values, preferred_element_type=F32)
    single = jnp.dot(expo_tan.astype(BF16), values[:, :HD], preferred_element_type=F32)
    if state is None:
        return peak, add, add_tan, pair, single
    return (
        peak,
        total * fade + add,
        total_tan * fade + add_tan,
        numer * jnp.concatenate([fade, fade], axis=1) + pair,
        numer_tan * fade + single,
    )


def finish(state):
    _, total, total_tan, numer, numer_tan = state
    inverse = 1.0 / jnp.sum(total, axis=1, keepdims=True)
    total_tan = jnp.sum(total_tan, axis=1, keepdims=True) * SCALE
    attended = numer[:, :HD] * inverse
    attended_tan = (numer_tan * SCALE + numer[:, HD:] - attended * total_tan) * inverse
    return attended.astype(BF16), attended_tan.astype(BF16)


def load_state(ref, rows):
    cut = [ref[rows, c * HD : (c + 1) * HD] for c in range(3)]
    return (*cut, ref[rows, 3 * HD : 5 * HD], ref[rows, 5 * HD :])


def attend_kernel(first, shared_ref, own_ref, shared_keys, own_keys, *refs):
    sides = ((shared_ref, shared_keys, refs[-2]), (own_ref, own_keys, refs[-1]))
    for side, (query, keys, out_ref) in enumerate(sides):
        state = None if first else load_state(refs[side], slice(None))
        out_ref[...] = jnp.concatenate(attend(query[...], keys, state), axis=1)


def attend_step(queries, keys, state):
    rows = [query.shape[0] for query in queries]
    return call(
        functools.partial(attend_kernel, not state),
        [jax.ShapeDtypeStruct((n, 6 * HD), F32) for n in rows],
        *queries,
        *keys,
        *state,
        flops=sum(rows) * keys[0].shape[0] * 1792,
    )


def attend_others_kernel(query_ref, keys, state_ref, *out_refs):
    rows = out_refs[0].shape[0] // 2
    most = slice(0, rows * len(out_refs))
    attended, attended_tan = finish(attend(query_ref[most, :], keys, load_state(state_ref, most)))
    for place, ref in enumerate(out_refs):
        ref[:rows, :] = attended[place * rows : (place + 1) * rows]
        ref[rows:, :] = attended_tan[place * rows : (place + 1) * rows]


def attend_kept_kernel(shared_ref, own_ref, shared_keys, own_keys, shared_state, own_state, out_ref):
    rows = own_ref.shape[0]
    start = shared_ref.shape[0] - rows
    sides = (
        (shared_ref, shared_keys, shared_state, slice(start, start + rows)),
        (own_ref, own_keys, own_state, slice(0, rows)),
    )
    for side, (query, keys, state, part) in enumerate(sides):
        lanes = slice(side * HD, (side + 1) * HD)
        attended, attended_tan = finish(attend(query[part, :], keys, load_state(state, part)))
        out_ref[:rows, lanes] = attended
        out_ref[rows:, lanes] = attended_tan


def cut_weight_kernel(y_ref, place_ref, w_ref, *refs):
    out_refs, sems = refs[:-1], refs[-1]
    columns = out_refs[0].shape[1]
    copies = []
    for flip in range(ZL * CORES):
        block = lax.bitwise_xor(place_ref[0], flip)
        lanes = pl.ds(pl.multiple_of(block * columns, HD), columns)
        for slot, k in enumerate(SLOTS):
            head = lax.rem(y_ref[0] + k, NY) if k < NY else NY
            source = w_ref.at[pl.ds(pl.multiple_of(head * HD, HD), HD), lanes]
            target = out_refs[flip].at[slot * HD : (slot + 1) * HD]
            copies.append(pltpu.make_async_copy(source, target, sems.at[flip, slot]))
    for copy in copies:
        copy.start()
    for copy in copies:
        copy.wait()


def project_sum(operands, terms, lanes=slice(None)):
    total = None
    for ref, low, high, weight, row in terms:
        part = jnp.dot(
            operands[ref][:, low:high],
            operands[weight][row : row + high - low, lanes],
            preferred_element_type=F32,
        )
        total = part if total is None else total + part
    return total


def project_kernel(terms, *refs):
    out_ref = refs[-1]
    total = project_sum(refs, terms)
    if len(refs) - 1 > 1 + max(term[3] for term in terms):
        total = total + refs[-2][...]
    out_ref[...] = total


def project_part(terms, *operands):
    shape = (operands[0].shape[0], operands[-1].shape[1])
    kernel = functools.partial(project_kernel, terms)
    return call(
        kernel,
        jax.ShapeDtypeStruct(shape, F32),
        *operands,
        flops=2 * shape[0] * shape[1] * sum(term[2] - term[1] for term in terms),
    )


def project_last_kernel(terms, *refs):
    operands, (out_ref, tan_ref, held_ref, sems) = refs[:-4], refs[-4:]
    rows, columns = out_ref.shape
    copies = []
    for place, start in enumerate(range(0, columns, 2 * HD)):
        lanes = slice(start, start + 2 * HD)
        total = operands[-1][:, lanes] + project_sum(operands, terms, lanes)
        held_ref[:, lanes] = total.astype(BF16)
        for half, ref in enumerate((out_ref, tan_ref)):
            source = held_ref.at[half * rows : (half + 1) * rows, lanes]
            copy = pltpu.make_async_copy(source, ref.at[:, lanes], sems.at[half, place])
            copy.start()
            copies.append(copy)
    for copy in copies:
        copy.wait()


def project_last(terms, *operands):
    rows, columns = operands[-1].shape
    return pl.pallas_call(
        functools.partial(project_last_kernel, terms),
        in_specs=[VMEM] * len(operands),
        out_specs=[HBM, HBM],
        out_shape=[jax.ShapeDtypeStruct((rows // 2, columns), BF16)] * 2,
        scratch_shapes=[
            pltpu.VMEM((rows, columns), BF16),
            pltpu.SemaphoreType.DMA((2, columns // (2 * HD))),
        ],
        name="project_last",
        compiler_params=pltpu.CompilerParams(vmem_limit_bytes=16 << 20),
    )(*operands)


def shard_step(queries, keys, values, query_tan, key_tan, value_tan, out_weight):
    rows, width = queries.shape
    heads = width // HD
    slab = keys.shape[0]
    columns = out_weight.shape[1] // (ZL * CORES)
    place = lax.axis_index("head").astype(jnp.int32).reshape(1)
    tok = lax.axis_index("tok").astype(jnp.int32).reshape(1)
    y = jnp.where(place % CORES == 0, tok % NY, tok // NY % NX)
    with_index = [SMEM] + [VMEM] * 8
    out_weight = pltpu.with_memory_space_constraint(out_weight, pltpu.HBM)
    keys, values, query_tan, key_tan, value_tan, queries = (
        pltpu.with_memory_space_constraint(array, pltpu.HBM)
        for array in (keys, values, query_tan, key_tan, value_tan, queries)
    )

    packed = call(
        pack_keys_kernel,
        jax.ShapeDtypeStruct((heads, slab, 4 * HD), BF16),
        keys,
        key_tan,
        values,
        value_tan,
        specs=[HBM] * 4,
        scratch_shapes=[pltpu.VMEM((4, slab, width), BF16), pltpu.SemaphoreType.DMA((4,))],
    )
    pieces = [packed] + [shift(packed, zh=k) for k in (1, 3, 2)]

    sends = call(
        pack_queries_kernel,
        [jax.ShapeDtypeStruct((rows, 2 * HD), BF16)] * (NY + 1),
        y,
        queries,
        query_tan,
        specs=[SMEM, HBM, HBM],
        scratch_shapes=[pltpu.VMEM((2, rows, width), BF16), pltpu.SemaphoreType.DMA((2,))],
    )
    others = [shift(sends[k], swap=k) for k in (1, 2, 3)]
    blocks = [jnp.concatenate([*others, sends[0]]), sends[NY]]

    place, _ = lax.optimization_barrier((place, sends[1]))
    cuts = call(
        cut_weight_kernel,
        [jax.ShapeDtypeStruct((width, columns), BF16)] * (ZL * CORES),
        y,
        place,
        out_weight,
        specs=[SMEM, SMEM, HBM],
        scratch_shapes=[pltpu.SemaphoreType.DMA((ZL * CORES, NY + 1))],
    )
    pieces, cuts = lax.optimization_barrier((pieces, cuts))

    split = call(
        split_keys_kernel,
        [jax.ShapeDtypeStruct((2 * ZH * slab, 4 * HD), BF16)] * NY,
        y,
        *pieces,
        specs=with_index[: ZH + 1],
    )
    cuts, _ = lax.optimization_barrier((cuts, split[0]))
    weight_near = shift(cuts[2], zl=1)
    weight_far = across(cuts[3])
    weight_core = shift(cuts[1], core=1)

    own = call(
        join_keys_kernel,
        [jax.ShapeDtypeStruct((NY * ZH * slab, 4 * HD), BF16)] * 2,
        split[0],
        *[shift(split[k], swap=k) for k in (1, 3, 2)],
    )
    left = [shift(own[0], ring=1), shift(own[1], ring=1)]
    right = [shift(own[0], ring=-1), shift(own[1], ring=-1)]
    opposite = [shift(left[0], ring=1), shift(right[1], ring=-1)]

    state = attend_step(blocks, own, ())
    state = attend_step(blocks, (left[0], right[1]), state)
    state = attend_step(blocks, (right[0], left[1]), state)
    others = call(
        attend_others_kernel,
        [jax.ShapeDtypeStruct((2 * rows, HD), BF16)] * (NY - 1),
        blocks[0],
        opposite[0],
        state[0],
        flops=3 * rows * opposite[0].shape[0] * 1792,
    )
    opposite[1], _ = lax.optimization_barrier((opposite[1], others[0]))
    kept = call(
        attend_kept_kernel,
        jax.ShapeDtypeStruct((2 * rows, 2 * HD), BF16),
        *blocks,
        *opposite,
        *state,
        flops=2 * rows * opposite[0].shape[0] * 1792,
    )

    near = [
        shift(kept, zl=1),
        jnp.concatenate([shift(others[k - 1], swap=-k, zl=1) for k in (1, 2, 3)], axis=1),
    ]
    mine = [kept, jnp.concatenate([shift(others[k - 1], swap=-k) for k in (1, 2, 3)], axis=1)]
    sibling = [shift(mine[n], core=1) for n in range(2)]
    far = [shift(near[n], core=1) for n in range(2)]
    own, rest = 2 * HD, 3 * HD
    partial = project_part(
        (
            (0, 0, own, 3, 0),
            (1, 0, own, 4, 0),
            (2, 0, rest, 5, own),
        ),
        mine[0],
        sibling[0],
        near[1],
        cuts[0],
        weight_core,
        weight_near,
    )
    partial = project_part(
        ((0, 0, rest, 3, own), (1, 0, rest, 4, own), (2, 0, own, 5, 0)),
        far[1],
        mine[1],
        near[0],
        weight_far,
        cuts[0],
        weight_near,
        partial,
    )
    return tuple(
        project_last(
            ((0, 0, rest, 2, own), (1, 0, own, 3, 0)),
            sibling[1],
            far[0],
            weight_core,
            weight_far,
            partial,
        )
    )


def solution(mesh):
    spec = P("tok", "head")
    return jax.shard_map(
        shard_step,
        mesh=mesh,
        in_specs=(spec,) * 6 + (P("head", None),),
        out_specs=(spec, spec),
        check_vma=False,
    )
```
